32 devices in a mesh: seq: 8 (over y, x, core), pipe: 4 (over z).
Axes of the slice: x: 2, y: 2, z: 4, core: 2. Of those that a mesh axis runs over, the one named last changes fastest.
Arguments:
- section_input: bfloat16 [4, 1024, 4096], P('pipe', 'seq'), may hold values from -6 to 6
- out_grad: bfloat16 [4, 1024, 4096], P('pipe', 'seq'), may hold values from -6 to 6
- conv_filter: float32 [4, 1024, 4096], P('pipe', None, 'seq'), may hold values from -2 to 2
- short_taps: float32 [4, 3, 3, 4096], P('pipe'), may hold values from -3 to 3
Outputs:
- grad_prev: bfloat16 [4, 1024, 4096], P('pipe', 'seq')
- filter_grad: float32 [4, 1024, 4096], P('pipe', None, 'seq')
The draws below stay inside these ranges and needn't reach their ends.
All inputs are finite; a program needn't handle non-finite values.
Results may differ from the reference program's by a relative error of at most 0.011.
Values may be sent and summed in bfloat16 or wider, within the bound.
No kernel may reach another device: no remote copies, remote signals or barrier semaphores. Data moves between devices by JAX's collectives and lax.ppermute only.
A program may use at most 128 MiB of HBM per device.

```python
import math
import jax
import jax.numpy as jnp

D = 4096
TAPS = 3
STREAMS = 3
SEQ = 1024
SECTIONS = 4


def draw_conv_filter(key, part):
    key_len, key_noise = jax.random.split(key, 2)
    positions = jnp.arange(SEQ, dtype=jnp.float32)[None, :, None]
    log_len = jax.random.uniform(key_len, (SECTIONS, 1, D), jnp.float32, math.log(30.0), math.log(2.0 * SEQ))
    noise = jnp.clip(jax.random.normal(key_noise, (SECTIONS, SEQ, D), jnp.float32), -6.0, 6.0)
    rates = jnp.exp(-log_len)
    amplitude = jnp.sqrt(2.0 * rates / (1.0 - jnp.exp(-2.0 * rates * SEQ)))
    return (amplitude * jnp.exp(-rates * positions) * noise).astype(jnp.float32)


def block_scale(key, dims, cuts, low, largest):
    level, own = 1.0, jax.random.fold_in(key, 6)
    for position, shards_of in cuts:
        heights = jnp.exp(jax.random.uniform(jax.random.fold_in(own, position), (shards_of,), jnp.float32, low / len(cuts), largest / len(cuts)))
        level = level * jnp.repeat(heights, dims[position] // shards_of).reshape([-1 if axis == position else 1 for axis in range(len(dims))])
    return level


def centred(rng, dims, spread, limit, cuts=(), kind=jnp.bfloat16):
    entries = jax.random.normal(rng, dims, jnp.float32) * spread
    if len(cuts) > 0:
        entries = block_scale(rng, dims, cuts, -0.22, 0.18) * entries
    return jnp.clip(entries, min=-limit, max=limit).astype(kind)


def setup_inputs(seed: int = 0) -> dict:
    streams_of = jax.random.split(jax.random.key(seed), 5)
    section_input = centred(streams_of[0], (SECTIONS, SEQ, D), 1.0, 6.0, ((0, 4), (1, 8)))
    out_grad = centred(streams_of[1], (SECTIONS, SEQ, D), 1.0, 6.0, ((0, 4), (1, 8)))
    conv_filter = draw_conv_filter(jax.random.fold_in(streams_of[4], 71), 0)
    short_taps = centred(streams_of[3], (SECTIONS, STREAMS, TAPS, D), 0.7, 3.0, ((0, 4),), jnp.float32)
    return {"section_input": section_input, "out_grad": out_grad, "conv_filter": conv_filter, "short_taps": short_taps}


def causal_mix(signal, weights):
    summed = jnp.zeros_like(signal)
    for tap_idx in range(TAPS):
        moved = jnp.pad(signal, ((tap_idx, 0), (0, 0)))[:SEQ]
        summed = summed + weights[tap_idx] * moved
    return summed

def adjoint_mix(signal, weights):
    summed = jnp.zeros_like(signal)
    for tap_idx in range(TAPS):
        moved = jnp.pad(signal, ((0, tap_idx), (0, 0)))[tap_idx:]
        summed = summed + weights[tap_idx] * moved
    return summed

def section_backward(inputs, upstream, kernel, tap_table):
    signal = inputs.astype(jnp.float32)
    query_rows = causal_mix(signal, tap_table[0]).astype(jnp.bfloat16)
    key_rows = causal_mix(signal, tap_table[1]).astype(jnp.bfloat16)
    value_rows = causal_mix(signal, tap_table[2]).astype(jnp.bfloat16)
    upstream_f = upstream.astype(jnp.float32)
    product = key_rows.astype(jnp.float32) * value_rows.astype(jnp.float32)
    adjoint = upstream_f * query_rows.astype(jnp.float32)
    length = 2 * SEQ
    spec_prod = jnp.fft.rfft(product, n=length, axis=0)
    spec_kernel = jnp.fft.rfft(kernel.astype(jnp.float32), n=length, axis=0)
    spec_adj = jnp.fft.rfft(adjoint, n=length, axis=0)
    combined = jnp.fft.irfft(spec_prod * spec_kernel, n=length, axis=0)[:SEQ].astype(jnp.float32)
    backward = jnp.fft.irfft(jnp.conj(spec_kernel) * spec_adj, n=length, axis=0)[:SEQ].astype(jnp.float32)
    filter_grad = jnp.fft.irfft(jnp.conj(spec_prod) * spec_adj, n=length, axis=0)[:SEQ].astype(jnp.float32)
    filter_grad = filter_grad / math.sqrt(SEQ)
    grad_query = (upstream_f * combined).astype(jnp.bfloat16)
    grad_key = (backward * value_rows.astype(jnp.float32)).astype(jnp.bfloat16)
    grad_value = (backward * key_rows.astype(jnp.float32)).astype(jnp.bfloat16)
    summed = adjoint_mix(grad_query.astype(jnp.float32), tap_table[0])
    summed = summed + adjoint_mix(grad_key.astype(jnp.float32), tap_table[1])
    summed = summed + adjoint_mix(grad_value.astype(jnp.float32), tap_table[2])
    return (summed.astype(jnp.bfloat16), filter_grad)

def reference(section_input, out_grad, conv_filter, short_taps):
    grads = []
    filters = []
    for section_idx in range(SECTIONS):
        grad_rows, filter_rows = section_backward(section_input[section_idx], out_grad[section_idx], conv_filter[section_idx], short_taps[section_idx])
        grads.append(grad_rows)
        filters.append(filter_rows)
    grad_stack = jnp.stack(grads, axis=0)
    grad_prev = jnp.roll(grad_stack, -1, axis=0)
    return (grad_prev, jnp.stack(filters, axis=0))
```

```python
import math

import jax
import jax.numpy as jnp
import numpy as np
from jax import lax
from jax.experimental import pallas as pl
from jax.experimental.pallas import tpu as pltpu
from jax.sharding import PartitionSpec as P

FREQ_BLOCK = 256
ROW_BLOCK = 256
STEP = 32
DENSE_ROWS = 1024
VMEM_BYTES = 56 * 1024 * 1024


def angle_tables(rows):
    def pair(outer, inner):
        angles = 2.0 * np.pi / (4 * rows) * (np.outer(outer, inner) % (4 * rows))
        return np.cos(angles), np.sin(angles)

    places = np.arange(rows)
    freqs = 4 * np.arange(rows) + 1
    coarse = STEP * np.arange(rows // STEP)
    fine = np.arange(STEP)
    by_place = pair(4 * coarse, places) + pair(4 * fine + 1, places)
    by_freq = pair(coarse, freqs) + pair(fine, freqs)
    return np.stack(by_place).astype(np.float32), np.stack(by_freq).astype(np.float32)


def turned(coarse_cos, coarse_sin, fine_cos, fine_sin):
    real = coarse_cos * fine_cos - coarse_sin * fine_sin
    imag = coarse_sin * fine_cos + coarse_cos * fine_sin
    return real, -imag


def table_kernel(place_ref, freq_ref, kernel_ref, fwd_ref, inv_ref, spec_ref, kernel_low):
    step = pl.program_id(0)
    rows = place_ref.shape[2]
    freq_block = fwd_ref.shape[0] // 2
    row_block = inv_ref.shape[0]

    @pl.when(step == 0)
    def _():
        kernel_low[...] = kernel_ref[...].astype(jnp.bfloat16)

    for part in range(freq_block // STEP):
        coarse = step * (freq_block // STEP) + part
        real, imag = turned(
            place_ref[0, pl.ds(coarse, 1), :],
            place_ref[1, pl.ds(coarse, 1), :],
            place_ref[2],
            place_ref[3],
        )
        fwd_ref[part * STEP : (part + 1) * STEP, :] = real.astype(jnp.bfloat16)
        fwd_ref[freq_block + part * STEP : freq_block + (part + 1) * STEP, :] = imag.astype(
            jnp.bfloat16
        )
    for part in range(row_block // STEP):
        coarse = step * (row_block // STEP) + part
        real, imag = turned(
            freq_ref[0, pl.ds(coarse, 1), :],
            freq_ref[1, pl.ds(coarse, 1), :],
            freq_ref[2],
            freq_ref[3],
        )
        real = (real * (1.0 / rows)).astype(jnp.bfloat16)
        imag = (imag * (1.0 / rows)).astype(jnp.bfloat16)
        for block in range(rows // freq_block):
            start = 2 * block * freq_block
            source = slice(block * freq_block, (block + 1) * freq_block)
            into = slice(part * STEP, (part + 1) * STEP)
            inv_ref[into, start : start + freq_block] = real[:, source]
            inv_ref[into, start + freq_block : start + 2 * freq_block] = imag[:, source]
    spec_ref[...] = jnp.dot(fwd_ref[...], kernel_low[...], preferred_element_type=jnp.float32)


def tables(kernel):
    rows, width = kernel.shape
    by_place, by_freq = angle_tables(rows)
    steps = rows // FREQ_BLOCK
    whole = lambda step: (0, 0, 0)
    return pl.pallas_call(
        table_kernel,
        grid=(steps,),
        in_specs=[
            pl.BlockSpec(by_place.shape, whole),
            pl.BlockSpec(by_freq.shape, whole),
            pl.BlockSpec((rows, width), lambda step: (0, 0)),
        ],
        out_specs=[
            pl.BlockSpec((2 * FREQ_BLOCK, rows), lambda step: (step, 0)),
            pl.BlockSpec((ROW_BLOCK, 2 * rows), lambda step: (step, 0)),
            pl.BlockSpec((2 * FREQ_BLOCK, width), lambda step: (step, 0)),
        ],
        out_shape=[
            jax.ShapeDtypeStruct((2 * rows, rows), jnp.bfloat16),
            jax.ShapeDtypeStruct((rows, 2 * rows), jnp.bfloat16),
            jax.ShapeDtypeStruct((2 * rows, width), jnp.float32),
        ],
        scratch_shapes=[pltpu.VMEM((rows, width), jnp.bfloat16)],
        compiler_params=pltpu.CompilerParams(vmem_limit_bytes=VMEM_BYTES),
        cost_estimate=pl.CostEstimate(
            flops=4 * rows * rows * width, bytes_accessed=16 * rows * rows, transcendentals=0
        ),
        name="tables",
    )(jnp.asarray(by_place), jnp.asarray(by_freq), kernel)


PAD = 8
CHUNK = 64


def section_kernel(
    x_ref, g_ref, tap_ref, fwd_ref, inv_ref, spec_ref,
    out_ref, filt_ref,
    padded, signals, key_rows, value_rows, mixed, later,
):
    step = pl.program_id(0)
    rows, width = x_ref.shape
    freq_block = fwd_ref.shape[0] // 2
    row_block = inv_ref.shape[0]
    freq_steps = rows // freq_block
    row_steps = rows // row_block

    @pl.when(step == 0)
    def _():
        padded[0:PAD, :] = jnp.zeros((PAD, width), jnp.float32)
        padded[PAD:, :] = x_ref[...].astype(jnp.float32)
        taps = [tap_ref[i : i + 1, :] for i in range(9)]

        @pl.loop(0, rows // CHUNK)
        def _(chunk):
            start = pl.multiple_of(chunk * CHUNK, CHUNK)
            window = padded[pl.ds(start, CHUNK + PAD), :]
            moved = [window[PAD - i : PAD - i + CHUNK, :] for i in range(3)]
            query, key, value = (
                (taps[3 * s] * moved[0] + taps[3 * s + 1] * moved[1] + taps[3 * s + 2] * moved[2])
                .astype(jnp.bfloat16)
                .astype(jnp.float32)
                for s in range(3)
            )
            here = pl.ds(start, CHUNK)
            key_rows[here, :] = key
            value_rows[here, :] = value
            signals[here, 0:width] = (key * value).astype(jnp.bfloat16)
            signals[here, width:] = (g_ref[here, :].astype(jnp.float32) * query).astype(
                jnp.bfloat16
            )

        later[...] = jnp.zeros(later.shape, jnp.float32)

    @pl.when(step < freq_steps)
    def _():
        both = jnp.dot(fwd_ref[...], signals[...], preferred_element_type=jnp.float32)
        p_re, p_im = both[:freq_block, :width], both[freq_block:, :width]
        a_re, a_im = both[:freq_block, width:], both[freq_block:, width:]
        h_re, h_im = spec_ref[:freq_block, :], spec_ref[freq_block:, :]
        start = pl.multiple_of(step * 2 * freq_block, 2 * freq_block)
        reals, imags = pl.ds(start, freq_block), pl.ds(start + freq_block, freq_block)
        mixed[reals, 0:width] = (p_re * h_re - p_im * h_im).astype(jnp.bfloat16)
        mixed[imags, 0:width] = (p_re * h_im + p_im * h_re).astype(jnp.bfloat16)
        mixed[reals, width : 2 * width] = (h_re * a_re + h_im * a_im).astype(jnp.bfloat16)
        mixed[imags, width : 2 * width] = (h_re * a_im - h_im * a_re).astype(jnp.bfloat16)
        mixed[reals, 2 * width :] = (p_re * a_re + p_im * a_im).astype(jnp.bfloat16)
        mixed[imags, 2 * width :] = (p_re * a_im - p_im * a_re).astype(jnp.bfloat16)

    @pl.when(step >= freq_steps)
    def _():
        block = row_steps - 1 - (step - freq_steps)
        start = pl.multiple_of(block * row_block, row_block)
        here = pl.ds(start, row_block)
        result = jnp.dot(inv_ref[...], mixed[...], preferred_element_type=jnp.float32)
        combined, backward = result[:, 0:width], result[:, width : 2 * width]
        filt_ref[...] = result[:, 2 * width :] * (1.0 / math.sqrt(rows))
        low = lambda v: v.astype(jnp.bfloat16).astype(jnp.float32)
        grads = (
            low(g_ref[here, :].astype(jnp.float32) * combined),
            low(backward * value_rows[here, :]),
            low(backward * key_rows[here, :]),
        )
        shifts = []
        for i in range(3):
            shifts.append(
                tap_ref[i : i + 1, :] * grads[0]
                + tap_ref[3 + i : 4 + i, :] * grads[1]
                + tap_ref[6 + i : 7 + i, :] * grads[2]
            )
        for i in (1, 2):
            later[i - 1, 0:row_block, :] = shifts[i]
        total = shifts[0] + later[0, 1 : 1 + row_block, :] + later[1, 2 : 2 + row_block, :]
        out_ref[...] = total.astype(jnp.bfloat16)
        for i in (1, 2):
            later[i - 1, row_block : row_block + PAD, :] = shifts[i][0:PAD, :]


def section(x, g, taps, fwd, inv, spec):
    rows, width = x.shape
    freq_steps, row_steps = rows // FREQ_BLOCK, rows // ROW_BLOCK
    forward = lambda step: (jnp.minimum(step, freq_steps - 1), 0)
    inverse = lambda step: (row_steps - 1 - jnp.maximum(step - freq_steps, 0), 0)
    once = lambda step: (0, 0)
    return pl.pallas_call(
        section_kernel,
        grid=(freq_steps + row_steps,),
        in_specs=[
            pl.BlockSpec((rows, width), once),
            pl.BlockSpec((rows, width), once),
            pl.BlockSpec(taps.shape, once),
            pl.BlockSpec((2 * FREQ_BLOCK, rows), forward),
            pl.BlockSpec((ROW_BLOCK, 2 * rows), inverse),
            pl.BlockSpec((2 * FREQ_BLOCK, width), forward),
        ],
        out_specs=[
            pl.BlockSpec((ROW_BLOCK, width), inverse),
            pl.BlockSpec((ROW_BLOCK, width), inverse),
        ],
        out_shape=[
            jax.ShapeDtypeStruct((rows, width), jnp.bfloat16),
            jax.ShapeDtypeStruct((rows, width), jnp.float32),
        ],
        scratch_shapes=[
            pltpu.VMEM((rows + PAD, width), jnp.float32),
            pltpu.VMEM((rows, 2 * width), jnp.bfloat16),
            pltpu.VMEM((rows, width), jnp.float32),
            pltpu.VMEM((rows, width), jnp.float32),
            pltpu.VMEM((2 * rows, 3 * width), jnp.bfloat16),
            pltpu.VMEM((2, ROW_BLOCK + PAD, width), jnp.float32),
        ],
        compiler_params=pltpu.CompilerParams(vmem_limit_bytes=VMEM_BYTES),
        cost_estimate=pl.CostEstimate(
            flops=20 * rows * rows * width,
            bytes_accessed=8 * rows * rows + 20 * rows * width,
            transcendentals=0,
        ),
        name="section",
    )(x, g, taps, fwd, inv, spec)


def phase_table(row_count, col_count, modulus, direction):
    row_ids = lax.broadcasted_iota(jnp.int32, (row_count, col_count), 0)
    col_ids = lax.broadcasted_iota(jnp.int32, (row_count, col_count), 1)
    residue = row_ids * col_ids % modulus
    angles = direction * 2.0 * math.pi / modulus * residue.astype(jnp.float32)
    return (jnp.cos(angles), jnp.sin(angles))


def highest(pattern, first_op, second_op):
    return jnp.einsum(pattern, first_op, second_op, precision=lax.Precision.HIGHEST)


def forward_spectrum(signal, half_q, width_p):
    full_q = 2 * half_q
    blocks = signal.reshape(half_q, width_p, signal.shape[1])
    fq_re, fq_im = phase_table(full_q, half_q, full_q, -1.0)
    section_re = highest("kq,qpc->kpc", fq_re, blocks)
    section_im = highest("kq,qpc->kpc", fq_im, blocks)
    tw_re, tw_im = phase_table(full_q, width_p, full_q * width_p, -1.0)
    turned_re = section_re * tw_re[:, :, None] - section_im * tw_im[:, :, None]
    turned_im = section_re * tw_im[:, :, None] + section_im * tw_re[:, :, None]
    fp_re, fp_im = phase_table(width_p, width_p, width_p, -1.0)
    out_re = highest("jp,kpc->jkc", fp_re, turned_re) - highest("jp,kpc->jkc", fp_im, turned_im)
    out_im = highest("jp,kpc->jkc", fp_re, turned_im) + highest("jp,kpc->jkc", fp_im, turned_re)
    return (out_re, out_im)


def inverse_field(spec_re, spec_im, half_q, width_p):
    full_q = 2 * half_q
    gp_re, gp_im = phase_table(width_p, width_p, width_p, 1.0)
    section_re = highest("mn,nqc->mqc", gp_re, spec_re) - highest("mn,nqc->mqc", gp_im, spec_im)
    section_im = highest("mn,nqc->mqc", gp_re, spec_im) + highest("mn,nqc->mqc", gp_im, spec_re)
    tw_re, tw_im = phase_table(width_p, full_q, full_q * width_p, 1.0)
    turned_re = section_re * tw_re[:, :, None] - section_im * tw_im[:, :, None]
    turned_im = section_re * tw_im[:, :, None] + section_im * tw_re[:, :, None]
    gq_re, gq_im = phase_table(half_q, full_q, full_q, 1.0)
    result = highest("aq,mqc->amc", gq_re, turned_re) - highest("aq,mqc->amc", gq_im, turned_im)
    return result.reshape(half_q * width_p, spec_re.shape[2]) / (full_q * width_p)


def large_section(x, g, taps, kernel, half_q):
    rows = x.shape[0]
    width_p = rows // half_q
    signal, upstream = x.astype(jnp.float32), g.astype(jnp.float32)
    moved = [jnp.pad(signal, ((i, 0), (0, 0)))[:rows] for i in range(3)]
    query, key, value = (
        sum(taps[3 * s + i] * moved[i] for i in range(3)).astype(jnp.bfloat16).astype(jnp.float32)
        for s in range(3)
    )
    p_re, p_im = forward_spectrum(key * value, half_q, width_p)
    a_re, a_im = forward_spectrum(upstream * query, half_q, width_p)
    h_re, h_im = forward_spectrum(kernel, half_q, width_p)
    combined = inverse_field(
        p_re * h_re - p_im * h_im, p_re * h_im + p_im * h_re, half_q, width_p
    )
    backward = inverse_field(
        h_re * a_re + h_im * a_im, h_re * a_im - h_im * a_re, half_q, width_p
    )
    filter_grad = inverse_field(
        p_re * a_re + p_im * a_im, p_re * a_im - p_im * a_re, half_q, width_p
    )
    grads = (upstream * combined, backward * value, backward * key)
    total = jnp.zeros_like(signal)
    for s in range(3):
        grad = grads[s].astype(jnp.bfloat16).astype(jnp.float32)
        for i in range(3):
            total = total + taps[3 * s + i] * jnp.pad(grad, ((0, i), (0, 0)))[i:]
    return total.astype(jnp.bfloat16), filter_grad * (1.0 / math.sqrt(rows))


def shards(section_input, out_grad, conv_filter, short_taps):
    inputs, upstream, kernel = section_input[0], out_grad[0], conv_filter[0]
    devices = lax.axis_size("seq")
    length_dev, model = inputs.shape
    rows, width = kernel.shape
    assert rows == length_dev * devices and model == width * devices
    me = lax.axis_index("seq")
    taps = lax.dynamic_slice_in_dim(short_taps[0].reshape(9, model), me * width, width, axis=1)
    to_columns = lambda block: block.reshape(length_dev, devices, width).transpose(1, 0, 2)
    sent = jnp.stack([to_columns(inputs), to_columns(upstream)], axis=1)
    got = lax.all_to_all(sent, "seq", split_axis=0, concat_axis=0, tiled=True)
    x_cols = got[:, 0].reshape(rows, width)
    g_cols = got[:, 1].reshape(rows, width)
    if rows <= DENSE_ROWS:
        fwd, inv, spec = tables(kernel)
        grad_cols, filter_grad = section(x_cols, g_cols, taps, fwd, inv, spec)
    else:
        grad_cols, filter_grad = large_section(x_cols, g_cols, taps, kernel, devices)
    back = lax.all_to_all(
        grad_cols.reshape(devices, length_dev, width), "seq", split_axis=0, concat_axis=0, tiled=True
    )
    grad_input = back.transpose(1, 0, 2).reshape(length_dev, model)
    count = lax.axis_size("pipe")
    received = lax.ppermute(
        grad_input[None], "pipe", [((i + 1) % count, i) for i in range(count)]
    )
    return received, filter_grad[None]


def solution(mesh):
    return jax.shard_map(
        shards,
        mesh=mesh,
        in_specs=(
            P("pipe", "seq", None),
            P("pipe", "seq", None),
            P("pipe", None, "seq"),
            P("pipe", None, None, None),
        ),
        out_specs=(P("pipe", "seq", None), P("pipe", None, "seq")),
        check_vma=False,
    )
```

```python
import functools
import math

import jax
import jax.numpy as jnp
import numpy as np
from jax import lax
from jax.experimental import pallas as pl
from jax.experimental.pallas import tpu as pltpu
from jax.sharding import PartitionSpec as P

FREQ_BLOCK = 256
ROW_BLOCK = 256
STEP = 32
DENSE_ROWS = 1024
VMEM_BYTES = 56 * 1024 * 1024


def angle_tables(rows):
    def pair(outer, inner):
        angles = 2.0 * np.pi / (4 * rows) * (np.outer(outer, inner) % (4 * rows))
        return np.cos(angles), np.sin(angles)

    places = np.arange(rows)
    freqs = 4 * np.arange(rows) + 1
    coarse = STEP * np.arange(rows // STEP)
    fine = np.arange(STEP)
    by_place = pair(4 * coarse, places) + pair(4 * fine + 1, places)
    by_freq = pair(coarse, freqs) + pair(fine, freqs)
    return np.stack(by_place).astype(np.float32), np.stack(by_freq).astype(np.float32)


def turned(coarse_cos, coarse_sin, fine_cos, fine_sin):
    real = coarse_cos * fine_cos - coarse_sin * fine_sin
    imag = coarse_sin * fine_cos + coarse_cos * fine_sin
    return real, -imag


def table_kernel(place_ref, freq_ref, kernel_ref, fwd_ref, inv_ref, spec_ref, kernel_low):
    step = pl.program_id(0)
    rows = place_ref.shape[2]
    freq_block = fwd_ref.shape[0] // 2
    row_block = inv_ref.shape[0]

    @pl.when(step == 0)
    def _():
        kernel_low[...] = kernel_ref[...].astype(jnp.bfloat16)

    for part in range(freq_block // STEP):
        coarse = step * (freq_block // STEP) + part
        real, imag = turned(
            place_ref[0, pl.ds(coarse, 1), :],
            place_ref[1, pl.ds(coarse, 1), :],
            place_ref[2],
            place_ref[3],
        )
        fwd_ref[part * STEP : (part + 1) * STEP, :] = real.astype(jnp.bfloat16)
        fwd_ref[freq_block + part * STEP : freq_block + (part + 1) * STEP, :] = imag.astype(
            jnp.bfloat16
        )
    for part in range(row_block // STEP):
        coarse = step * (row_block // STEP) + part
        real, imag = turned(
            freq_ref[0, pl.ds(coarse, 1), :],
            freq_ref[1, pl.ds(coarse, 1), :],
            freq_ref[2],
            freq_ref[3],
        )
        real = (real * (1.0 / rows)).astype(jnp.bfloat16)
        imag = (imag * (1.0 / rows)).astype(jnp.bfloat16)
        for block in range(rows // freq_block):
            start = 2 * block * freq_block
            source = slice(block * freq_block, (block + 1) * freq_block)
            into = slice(part * STEP, (part + 1) * STEP)
            inv_ref[into, start : start + freq_block] = real[:, source]
            inv_ref[into, start + freq_block : start + 2 * freq_block] = imag[:, source]
    spec_ref[...] = jnp.dot(fwd_ref[...], kernel_low[...], preferred_element_type=jnp.float32)


def tables(kernel):
    rows, width = kernel.shape
    by_place, by_freq = angle_tables(rows)
    steps = rows // FREQ_BLOCK
    whole = lambda step: (0, 0, 0)
    return pl.pallas_call(
        table_kernel,
        grid=(steps,),
        in_specs=[
            pl.BlockSpec(by_place.shape, whole),
            pl.BlockSpec(by_freq.shape, whole),
            pl.BlockSpec((rows, width), lambda step: (0, 0)),
        ],
        out_specs=[
            pl.BlockSpec((2 * FREQ_BLOCK, rows), lambda step: (step, 0)),
            pl.BlockSpec((ROW_BLOCK, 2 * rows), lambda step: (step, 0)),
            pl.BlockSpec((2 * FREQ_BLOCK, width), lambda step: (step, 0)),
        ],
        out_shape=[
            jax.ShapeDtypeStruct((2 * rows, rows), jnp.bfloat16),
            jax.ShapeDtypeStruct((rows, 2 * rows), jnp.bfloat16),
            jax.ShapeDtypeStruct((2 * rows, width), jnp.float32),
        ],
        scratch_shapes=[pltpu.VMEM((rows, width), jnp.bfloat16)],
        compiler_params=pltpu.CompilerParams(vmem_limit_bytes=VMEM_BYTES),
        cost_estimate=pl.CostEstimate(
            flops=4 * rows * rows * width, bytes_accessed=16 * rows * rows, transcendentals=0
        ),
        name="tables",
    )(jnp.asarray(by_place), jnp.asarray(by_freq), kernel)


PAD = 8
CHUNK = 64


def in_then_out(moves, held, in_sem, out_sem):
    arriving = [pltpu.make_async_copy(a, held.at[i], in_sem.at[i]) for i, (a, _) in enumerate(moves)]
    leaving = [pltpu.make_async_copy(held.at[i], b, out_sem.at[i]) for i, (_, b) in enumerate(moves)]
    for copy in arriving:
        copy.start()
    for first, second in zip(arriving, leaving):
        first.wait()
        second.start()
    for copy in leaving:
        copy.wait()


def pack_kernel(x_ref, g_ref, *refs):
    pieces, scratch = refs[:-3], refs[-3:]
    devices = lax.axis_size("seq")
    width = pieces[0].shape[2]
    chunks = len(pieces) // devices
    me = lax.axis_index("seq")
    moves = []
    for number, piece in enumerate(pieces):
        chunk, k = divmod(number, devices)
        start = pl.multiple_of(((me ^ k) * chunks + chunk) * width, width)
        for half, ref in enumerate((x_ref, g_ref)):
            moves.append((ref.at[:, pl.ds(start, width)], piece.at[half]))
    in_then_out(moves, *scratch)


def pack(x, g, devices, chunks):
    length, model = x.shape
    width = model // devices // chunks
    count = devices * chunks
    anywhere = pl.BlockSpec(memory_space=pl.ANY)
    pieces = pl.pallas_call(
        pack_kernel,
        in_specs=[anywhere] * 2,
        out_specs=[anywhere] * count,
        out_shape=[jax.ShapeDtypeStruct((2, length, width), x.dtype)] * count,
        scratch_shapes=[
            pltpu.VMEM((2 * count, length, width), x.dtype),
            pltpu.SemaphoreType.DMA((2 * count,)),
            pltpu.SemaphoreType.DMA((2 * count,)),
        ],
        name="pack",
    )(x, g)
    return [pieces[c * devices : (c + 1) * devices] for c in range(chunks)]


def unpack_kernel(*refs):
    pieces, out_ref, scratch = refs[:-4], refs[-4], refs[-3:]
    devices = lax.axis_size("seq")
    width = pieces[0].shape[1]
    chunks = len(pieces) // devices
    me = lax.axis_index("seq")
    moves = []
    for number, piece in enumerate(pieces):
        chunk, k = divmod(number, devices)
        start = pl.multiple_of(((me ^ k) * chunks + chunk) * width, width)
        moves.append((piece, out_ref.at[0, :, pl.ds(start, width)]))
    in_then_out(moves, *scratch)


def unpack(pieces):
    flat = [piece for chunk in pieces for piece in chunk]
    length, width = flat[0].shape
    anywhere = pl.BlockSpec(memory_space=pl.ANY)
    return pl.pallas_call(
        unpack_kernel,
        in_specs=[anywhere] * len(flat),
        out_specs=anywhere,
        out_shape=jax.ShapeDtypeStruct((1, length, width * len(flat)), flat[0].dtype),
        scratch_shapes=[
            pltpu.VMEM((len(flat), length, width), flat[0].dtype),
            pltpu.SemaphoreType.DMA((len(flat),)),
            pltpu.SemaphoreType.DMA((len(flat),)),
        ],
        name="unpack",
    )(*flat)


def section_kernel(devices, aliased, *refs):
    pieces, refs = refs[:devices], refs[devices:]
    tap_ref, fwd_ref, inv_ref, spec_ref = refs[:4]
    refs = refs[4 + aliased :]
    outs, refs = refs[:devices], refs[devices:]
    filt_ref, padded, upstream, signals, key_rows, value_rows, mixed, later, grad_rows = refs
    step = pl.program_id(0)
    me = lax.axis_index("seq")
    length, width = outs[0].shape
    rows = length * devices
    freq_block = fwd_ref.shape[0] // 2
    row_block = inv_ref.shape[0]
    freq_steps = rows // freq_block
    row_steps = rows // row_block
    place = lambda k, offset: pl.ds(pl.multiple_of((me ^ k) * length + offset, 8), length)

    @pl.when(step == 0)
    def _():
        padded[0:PAD, :] = jnp.zeros((PAD, width), jnp.float32)
        for k in range(devices):
            padded[place(k, PAD), :] = pieces[k][0].astype(jnp.float32)
            upstream[place(k, 0), :] = pieces[k][1].astype(jnp.float32)
        taps = [tap_ref[i : i + 1, :] for i in range(9)]

        @pl.loop(0, rows // CHUNK)
        def _(chunk):
            start = pl.multiple_of(chunk * CHUNK, CHUNK)
            window = padded[pl.ds(start, CHUNK + PAD), :]
            moved = [window[PAD - i : PAD - i + CHUNK, :] for i in range(3)]
            query, key, value = (
                (taps[3 * s] * moved[0] + taps[3 * s + 1] * moved[1] + taps[3 * s + 2] * moved[2])
                .astype(jnp.bfloat16)
                .astype(jnp.float32)
                for s in range(3)
            )
            here = pl.ds(start, CHUNK)
            key_rows[here, :] = key
            value_rows[here, :] = value
            signals[here, 0:width] = (key * value).astype(jnp.bfloat16)
            signals[here, width:] = (upstream[here, :] * query).astype(jnp.bfloat16)

        later[...] = jnp.zeros(later.shape, jnp.float32)

    @pl.when(step < freq_steps)
    def _():
        both = jnp.dot(fwd_ref[...], signals[...], preferred_element_type=jnp.float32)
        p_re, p_im = both[:freq_block, :width], both[freq_block:, :width]
        a_re, a_im = both[:freq_block, width:], both[freq_block:, width:]
        h_re, h_im = spec_ref[:freq_block, :], spec_ref[freq_block:, :]
        start = pl.multiple_of(step * 2 * freq_block, 2 * freq_block)
        reals, imags = pl.ds(start, freq_block), pl.ds(start + freq_block, freq_block)
        mixed[reals, 0:width] = (p_re * h_re - p_im * h_im).astype(jnp.bfloat16)
        mixed[imags, 0:width] = (p_re * h_im + p_im * h_re).astype(jnp.bfloat16)
        mixed[reals, width : 2 * width] = (h_re * a_re + h_im * a_im).astype(jnp.bfloat16)
        mixed[imags, width : 2 * width] = (h_re * a_im - h_im * a_re).astype(jnp.bfloat16)
        mixed[reals, 2 * width :] = (p_re * a_re + p_im * a_im).astype(jnp.bfloat16)
        mixed[imags, 2 * width :] = (p_re * a_im - p_im * a_re).astype(jnp.bfloat16)

    @pl.when(step >= freq_steps)
    def _():
        block = row_steps - 1 - (step - freq_steps)
        start = pl.multiple_of(block * row_block, row_block)
        here = pl.ds(start, row_block)
        result = jnp.dot(inv_ref[...], mixed[...], preferred_element_type=jnp.float32)
        combined, backward = result[:, 0:width], result[:, width : 2 * width]
        filt_ref[...] = result[:, 2 * width :] * (1.0 / math.sqrt(rows))
        low = lambda v: v.astype(jnp.bfloat16).astype(jnp.float32)
        grads = (
            low(upstream[here, :] * combined),
            low(backward * value_rows[here, :]),
            low(backward * key_rows[here, :]),
        )
        shifts = [
            tap_ref[i : i + 1, :] * grads[0]
            + tap_ref[3 + i : 4 + i, :] * grads[1]
            + tap_ref[6 + i : 7 + i, :] * grads[2]
            for i in range(3)
        ]
        for i in (1, 2):
            later[i - 1, 0:row_block, :] = shifts[i]
        total = shifts[0] + later[0, 1 : 1 + row_block, :] + later[1, 2 : 2 + row_block, :]
        grad_rows[here, :] = total.astype(jnp.bfloat16)
        for i in (1, 2):
            later[i - 1, row_block : row_block + PAD, :] = shifts[i][0:PAD, :]

    @pl.when(step == freq_steps + row_steps - 1)
    def _():
        for k in range(devices):
            outs[k][...] = grad_rows[place(k, 0), :]


def section(pieces, taps, fwd, inv, spec, chunk, filt):
    devices = len(pieces)
    length, width = pieces[0].shape[1:]
    rows = devices * length
    freq_steps, row_steps = rows // FREQ_BLOCK, rows // ROW_BLOCK
    forward = lambda step: (jnp.minimum(step, freq_steps - 1), 0)
    backward = lambda step: (row_steps - 1 - jnp.maximum(step - freq_steps, 0), 0)
    here = lambda index: lambda step: (index(step)[0], chunk)
    once = lambda step: (0, 0)
    more = [] if filt is None else [filt]
    *outs, filt = pl.pallas_call(
        functools.partial(section_kernel, devices, len(more)),
        grid=(freq_steps + row_steps,),
        in_specs=[pl.BlockSpec((2, length, width), lambda step: (0, 0, 0))] * devices
        + [
            pl.BlockSpec((taps.shape[0], width), lambda step: (0, chunk)),
            pl.BlockSpec((2 * FREQ_BLOCK, rows), forward),
            pl.BlockSpec((ROW_BLOCK, 2 * rows), backward),
            pl.BlockSpec((2 * FREQ_BLOCK, width), here(forward)),
        ]
        + [pl.BlockSpec(memory_space=pl.ANY)] * len(more),
        out_specs=[pl.BlockSpec((length, width), once)] * devices
        + [pl.BlockSpec((ROW_BLOCK, width), here(backward))],
        out_shape=[jax.ShapeDtypeStruct((length, width), jnp.bfloat16)] * devices
        + [jax.ShapeDtypeStruct((rows, taps.shape[1]), jnp.float32)],
        scratch_shapes=[
            pltpu.VMEM((rows + PAD, width), jnp.float32),
            pltpu.VMEM((rows, width), jnp.float32),
            pltpu.VMEM((rows, 2 * width), jnp.bfloat16),
            pltpu.VMEM((rows, width), jnp.float32),
            pltpu.VMEM((rows, width), jnp.float32),
            pltpu.VMEM((2 * rows, 3 * width), jnp.bfloat16),
            pltpu.VMEM((2, ROW_BLOCK + PAD, width), jnp.float32),
            pltpu.VMEM((rows, width), jnp.bfloat16),
        ],
        input_output_aliases={devices + 4: devices} if more else {},
        compiler_params=pltpu.CompilerParams(vmem_limit_bytes=VMEM_BYTES),
        cost_estimate=pl.CostEstimate(
            flops=20 * rows * rows * width,
            bytes_accessed=8 * rows * rows + 20 * rows * width,
            transcendentals=0,
        ),
        name="section",
    )(*pieces, taps, fwd, inv, spec, *more)
    return outs, filt


def phase_table(row_count, col_count, modulus, direction):
    row_ids = lax.broadcasted_iota(jnp.int32, (row_count, col_count), 0)
    col_ids = lax.broadcasted_iota(jnp.int32, (row_count, col_count), 1)
    residue = row_ids * col_ids % modulus
    angles = direction * 2.0 * math.pi / modulus * residue.astype(jnp.float32)
    return (jnp.cos(angles), jnp.sin(angles))


def highest(pattern, first_op, second_op):
    return jnp.einsum(pattern, first_op, second_op, precision=lax.Precision.HIGHEST)


def forward_spectrum(signal, half_q, width_p):
    full_q = 2 * half_q
    blocks = signal.reshape(half_q, width_p, signal.shape[1])
    fq_re, fq_im = phase_table(full_q, half_q, full_q, -1.0)
    section_re = highest("kq,qpc->kpc", fq_re, blocks)
    section_im = highest("kq,qpc->kpc", fq_im, blocks)
    tw_re, tw_im = phase_table(full_q, width_p, full_q * width_p, -1.0)
    turned_re = section_re * tw_re[:, :, None] - section_im * tw_im[:, :, None]
    turned_im = section_re * tw_im[:, :, None] + section_im * tw_re[:, :, None]
    fp_re, fp_im = phase_table(width_p, width_p, width_p, -1.0)
    out_re = highest("jp,kpc->jkc", fp_re, turned_re) - highest("jp,kpc->jkc", fp_im, turned_im)
    out_im = highest("jp,kpc->jkc", fp_re, turned_im) + highest("jp,kpc->jkc", fp_im, turned_re)
    return (out_re, out_im)


def inverse_field(spec_re, spec_im, half_q, width_p):
    full_q = 2 * half_q
    gp_re, gp_im = phase_table(width_p, width_p, width_p, 1.0)
    section_re = highest("mn,nqc->mqc", gp_re, spec_re) - highest("mn,nqc->mqc", gp_im, spec_im)
    section_im = highest("mn,nqc->mqc", gp_re, spec_im) + highest("mn,nqc->mqc", gp_im, spec_re)
    tw_re, tw_im = phase_table(width_p, full_q, full_q * width_p, 1.0)
    turned_re = section_re * tw_re[:, :, None] - section_im * tw_im[:, :, None]
    turned_im = section_re * tw_im[:, :, None] + section_im * tw_re[:, :, None]
    gq_re, gq_im = phase_table(half_q, full_q, full_q, 1.0)
    result = highest("aq,mqc->amc", gq_re, turned_re) - highest("aq,mqc->amc", gq_im, turned_im)
    return result.reshape(half_q * width_p, spec_re.shape[2]) / (full_q * width_p)


def large_section(x, g, taps, kernel, half_q):
    rows = x.shape[0]
    width_p = rows // half_q
    signal, upstream = x.astype(jnp.float32), g.astype(jnp.float32)
    moved = [jnp.pad(signal, ((i, 0), (0, 0)))[:rows] for i in range(3)]
    query, key, value = (
        sum(taps[3 * s + i] * moved[i] for i in range(3)).astype(jnp.bfloat16).astype(jnp.float32)
        for s in range(3)
    )
    p_re, p_im = forward_spectrum(key * value, half_q, width_p)
    a_re, a_im = forward_spectrum(upstream * query, half_q, width_p)
    h_re, h_im = forward_spectrum(kernel, half_q, width_p)
    combined = inverse_field(
        p_re * h_re - p_im * h_im, p_re * h_im + p_im * h_re, half_q, width_p
    )
    backward = inverse_field(
        h_re * a_re + h_im * a_im, h_re * a_im - h_im * a_re, half_q, width_p
    )
    filter_grad = inverse_field(
        p_re * a_re + p_im * a_im, p_re * a_im - p_im * a_re, half_q, width_p
    )
    grads = (upstream * combined, backward * value, backward * key)
    total = jnp.zeros_like(signal)
    for s in range(3):
        grad = grads[s].astype(jnp.bfloat16).astype(jnp.float32)
        for i in range(3):
            total = total + taps[3 * s + i] * jnp.pad(grad, ((0, i), (0, 0)))[i:]
    return total.astype(jnp.bfloat16), filter_grad * (1.0 / math.sqrt(rows))


CHUNKS = 1


def fast(inputs, upstream, kernel, taps):
    devices, count = lax.axis_size("seq"), lax.axis_size("pipe")
    pieces = pack(inputs, upstream, devices, CHUNKS)
    across = lambda k: [(i, i ^ k) for i in range(devices)]
    home = lambda k: [
        (i * count + p, (i ^ k) * count + (p - 1) % count)
        for i in range(devices)
        for p in range(count)
    ]
    arrived = [
        [chunk[0]] + [lax.ppermute(chunk[k], "seq", across(k)) for k in range(1, devices)]
        for chunk in pieces
    ]
    fwd, inv, spec = tables(kernel)
    filter_grad, grads = None, []
    for chunk in range(CHUNKS):
        outs, filter_grad = section(arrived[chunk], taps, fwd, inv, spec, chunk, filter_grad)
        grads.append([lax.ppermute(outs[k], ("seq", "pipe"), home(k)) for k in range(devices)])
    return unpack(grads), filter_grad[None]


def general(inputs, upstream, kernel, taps):
    devices, count = lax.axis_size("seq"), lax.axis_size("pipe")
    length_dev, model = inputs.shape
    rows, width = kernel.shape
    to_columns = lambda block: block.reshape(length_dev, devices, width).transpose(1, 0, 2)
    sent = jnp.stack([to_columns(inputs), to_columns(upstream)], axis=1)
    got = lax.all_to_all(sent, "seq", split_axis=0, concat_axis=0, tiled=True)
    x_cols, g_cols = got[:, 0].reshape(rows, width), got[:, 1].reshape(rows, width)
    grad_cols, filter_grad = large_section(x_cols, g_cols, taps, kernel, devices)
    back = lax.all_to_all(
        grad_cols.reshape(devices, length_dev, width), "seq", split_axis=0, concat_axis=0, tiled=True
    )
    grad_input = back.transpose(1, 0, 2).reshape(length_dev, model)
    received = lax.ppermute(
        grad_input[None], "pipe", [((i + 1) % count, i) for i in range(count)]
    )
    return received, filter_grad[None]


def shards(section_input, out_grad, conv_filter, short_taps):
    inputs, upstream, kernel = section_input[0], out_grad[0], conv_filter[0]
    devices = lax.axis_size("seq")
    model = inputs.shape[1]
    rows, width = kernel.shape
    taps = lax.dynamic_slice_in_dim(
        short_taps[0].reshape(-1, model), lax.axis_index("seq") * width, width, axis=1
    )
    dense = (
        rows <= DENSE_ROWS
        and rows % FREQ_BLOCK == 0
        and width % (CHUNKS * 128) == 0
        and devices & (devices - 1) == 0
    )
    return (fast if dense else general)(inputs, upstream, kernel, taps)


def solution(mesh):
    return jax.shard_map(
        shards,
        mesh=mesh,
        in_specs=(
            P("pipe", "seq", None),
            P("pipe", "seq", None),
            P("pipe", None, "seq"),
            P("pipe", None, None, None),
        ),
        out_specs=(P("pipe", "seq", None), P("pipe", None, "seq")),
        check_vma=False,
    )
```

```python
import functools
import math

import jax
import jax.numpy as jnp
import numpy as np
from jax import lax
from jax.experimental import pallas as pl
from jax.experimental.pallas import tpu as pltpu
from jax.sharding import PartitionSpec as P

WHOLE_IN = (False, False)
WHOLE_OUT = (True, False)
CHUNKS = len(WHOLE_IN)
PAD = 8
TILE = 16
LAST_TILE = 64
DENSE_ROWS = 1024
SPECTRUM_VMEM = 12 * 1024 * 1024
SECTION_VMEM = 28 * 1024 * 1024
COS = [math.cos(math.pi / 8 * j) for j in range(4)]
SIN = [math.sin(math.pi / 8 * j) for j in range(4)]


def quarter_tables(rows):
    quarter = rows // 4
    freqs = 16 * np.arange(quarter)[None, :, None] + 4 * np.arange(4)[:, None, None] + 1
    angles = 2.0 * np.pi / (4 * rows) * (freqs * np.arange(quarter) % (4 * rows))
    real, imag = np.cos(angles), -np.sin(angles)
    fwd = np.concatenate(
        [np.concatenate([real, -imag], axis=2), np.concatenate([imag, real], axis=2)], axis=1
    )
    inv = np.swapaxes(fwd, 1, 2) / rows
    return jnp.asarray(fwd.astype(jnp.bfloat16)), jnp.asarray(inv.astype(jnp.bfloat16))


def split(x0, x1, x2, x3):
    even, turn = x0 + COS[2] * x2, SIN[2] * x2
    odd = x0 - COS[2] * x2
    sum_re, sum_im = COS[1] * x1 + COS[3] * x3, SIN[1] * x1 + SIN[3] * x3
    dif_re, dif_im = COS[1] * x1 - COS[3] * x3, SIN[1] * x1 - SIN[3] * x3
    return (
        (even + sum_re, -turn - sum_im),
        (odd - dif_im, turn - dif_re),
        (even - sum_re, sum_im - turn),
        (odd + dif_im, turn + dif_re),
    )


def joined(v0, v1, v2, v3):
    a_re, a_im, b_re, b_im = v0[0] + v2[0], v0[1] + v2[1], v1[0] + v3[0], v1[1] + v3[1]
    c_re, c_im, d_re, d_im = v0[0] - v2[0], v0[1] - v2[1], v1[0] - v3[0], v1[1] - v3[1]
    return (
        a_re + b_re,
        COS[1] * (c_re - d_im) - SIN[1] * (c_im + d_re),
        COS[2] * (a_re - b_re) - SIN[2] * (a_im - b_im),
        COS[3] * (c_re + d_im) - SIN[3] * (c_im - d_re),
    )


def by_target(refs, devices, whole):
    me, refs = lax.axis_index("seq"), list(refs)
    pairs = []
    for together in whole:
        if together:
            ref = refs.pop(0)
            pairs.append([(d, ref.at[d]) for d in range(devices)])
        else:
            pairs.append([(me ^ k, refs.pop(0)) for k in range(devices)])
    return pairs


def pack_kernel(whole, x_ref, g_ref, *refs):
    pieces, sem = refs[:-1], refs[-1]
    devices = lax.axis_size("seq")
    width = pieces[0].shape[-1]
    copies = []
    for chunk, pairs in enumerate(by_target(pieces, devices, whole)):
        for number, (device, piece) in enumerate(pairs):
            start = pl.multiple_of((device * len(whole) + chunk) * width, width)
            for half, ref in enumerate((x_ref, g_ref)):
                copies.append(
                    pltpu.make_async_copy(
                        ref.at[:, pl.ds(start, width)],
                        piece.at[half],
                        sem.at[chunk * devices + number, half],
                    )
                )
    for copy in copies:
        copy.start()
    for copy in copies:
        copy.wait()


def pack(x, g, devices, whole):
    length, model = x.shape
    width = model // devices // len(whole)
    shapes = []
    for together in whole:
        shapes += [(devices, 2, length, width)] if together else [(2, length, width)] * devices
    pieces = pl.pallas_call(
        functools.partial(pack_kernel, whole),
        in_specs=[pl.BlockSpec(memory_space=pl.ANY)] * 2,
        out_specs=[pl.BlockSpec(memory_space=pltpu.VMEM)] * len(shapes),
        out_shape=[jax.ShapeDtypeStruct(shape, x.dtype) for shape in shapes],
        scratch_shapes=[pltpu.SemaphoreType.DMA((devices * len(whole), 2))],
        compiler_params=pltpu.CompilerParams(vmem_limit_bytes=8 * 1024 * 1024),
        name="pack",
    )(x, g)
    chunks, pieces = [], list(pieces)
    for together in whole:
        taken = 1 if together else devices
        chunks.append(pieces[:taken])
        pieces = pieces[taken:]
    return chunks


def unpack_kernel(whole, *refs):
    pieces, out_ref, sem = refs[:-2], refs[-2], refs[-1]
    devices = lax.axis_size("seq")
    width = pieces[0].shape[-1]
    copies = []
    for chunk, pairs in enumerate(by_target(pieces, devices, whole)):
        for number, (device, piece) in enumerate(pairs):
            start = pl.multiple_of((device * len(whole) + chunk) * width, width)
            copies.append(
                pltpu.make_async_copy(
                    piece,
                    out_ref.at[0, :, pl.ds(start, width)],
                    sem.at[chunk * devices + number],
                )
            )
    for copy in copies:
        copy.start()
    for copy in copies:
        copy.wait()


def unpack(chunks, devices, whole):
    flat = [piece for chunk in chunks for piece in chunk]
    length, width = flat[0].shape[-2:]
    count = devices * len(whole)
    return pl.pallas_call(
        functools.partial(unpack_kernel, whole),
        in_specs=[pl.BlockSpec(memory_space=pltpu.VMEM)] * len(flat),
        out_specs=pl.BlockSpec(memory_space=pl.ANY),
        out_shape=jax.ShapeDtypeStruct((1, length, width * count), flat[0].dtype),
        scratch_shapes=[pltpu.SemaphoreType.DMA((count,))],
        compiler_params=pltpu.CompilerParams(vmem_limit_bytes=8 * 1024 * 1024),
        name="unpack",
    )(*flat)


def spectrum_kernel(kernel_ref, fwd_ref, spec_ref, turned):
    rows = kernel_ref.shape[0]
    quarter = rows // 4

    @pl.loop(0, quarter // TILE)
    def _(step):
        start = pl.multiple_of(step * TILE, TILE)
        parts = split(*(kernel_ref[pl.ds(start + j * quarter, TILE), :] for j in range(4)))
        for j, (real, imag) in enumerate(parts):
            turned[j, pl.ds(start, TILE), :] = real.astype(jnp.bfloat16)
            turned[j, pl.ds(start + quarter, TILE), :] = imag.astype(jnp.bfloat16)

    for j in range(4):
        spec_ref[j] = jnp.dot(fwd_ref[j], turned[j], preferred_element_type=jnp.float32)


def spectrum(kernel, fwd):
    rows, width = kernel.shape
    near = pl.BlockSpec(memory_space=pltpu.VMEM)
    return pl.pallas_call(
        spectrum_kernel,
        in_specs=[near] * 2,
        out_specs=near,
        out_shape=jax.ShapeDtypeStruct((4, rows // 2, width), jnp.float32),
        scratch_shapes=[pltpu.VMEM((4, rows // 2, width), jnp.bfloat16)],
        compiler_params=pltpu.CompilerParams(vmem_limit_bytes=SPECTRUM_VMEM),
        cost_estimate=pl.CostEstimate(
            flops=2 * rows * rows * width, bytes_accessed=14 * rows * width, transcendentals=0
        ),
        name="spectrum",
    )(kernel, fwd)


def section_kernel(devices, chunk, aliased, whole_in, whole_out, *refs):
    taken = 1 if whole_in else devices
    (pieces,) = by_target(refs[:taken], devices, [whole_in])
    refs = refs[taken:]
    tap_ref, fwd_ref, inv_ref, spec_ref = refs[:4]
    refs = refs[4 + aliased :]
    out_ref, filt_ref, padded, upstream, key_rows, value_rows, turned, mixed, back = refs[:9]
    shifted_rows, filt_rows, grad_rows, tap_rows, filt_sem, tap_sem = refs[9:]
    me = lax.axis_index("seq")
    length, width = pieces[0][1].shape[1:]
    rows = length * devices
    quarter = rows // 4
    columns = slice(chunk * width, (chunk + 1) * width)
    place = lambda device, offset: pl.ds(pl.multiple_of(device * length + offset, 8), length)
    low = lambda v: v.astype(jnp.bfloat16).astype(jnp.float32)

    start = pl.multiple_of((me * (spec_ref.shape[2] // width) + chunk) * width, width)
    fetch = pltpu.make_async_copy(tap_ref.at[0, :, :, pl.ds(start, width)], tap_rows, tap_sem)
    fetch.start()
    padded[0:PAD, :] = jnp.zeros((PAD, width), jnp.float32)
    for device, piece in pieces:
        padded[place(device, PAD), :] = piece[0].astype(jnp.float32)
        upstream[place(device, 0), :] = piece[1].astype(jnp.float32)
    fetch.wait()
    taps = [tap_rows[s, i : i + 1, :] for s in range(3) for i in range(3)]

    @pl.loop(0, quarter // TILE)
    def _(step):
        begin = pl.multiple_of(step * TILE, TILE)
        products, adjoints = [], []
        for j in range(4):
            here = pl.ds(begin + j * quarter, TILE)
            window = padded[pl.ds(begin + j * quarter, TILE + PAD), :]
            moved = [window[PAD - i : PAD - i + TILE, :] for i in range(3)]
            query, key, value = (
                low(sum(taps[3 * s + i] * moved[i] for i in range(3))) for s in range(3)
            )
            key_rows[here, :] = key
            value_rows[here, :] = value
            products.append(key * value)
            adjoints.append(upstream[here, :] * query)
        for half, signals in enumerate((products, adjoints)):
            into = slice(half * width, (half + 1) * width)
            for j, (real, imag) in enumerate(split(*signals)):
                turned[j, pl.ds(begin, TILE), into] = real.astype(jnp.bfloat16)
                turned[j, pl.ds(begin + quarter, TILE), into] = imag.astype(jnp.bfloat16)

    for j in range(4):
        both = jnp.dot(fwd_ref[j], turned[j], preferred_element_type=jnp.float32)
        p_re, p_im = both[:quarter, :width], both[quarter:, :width]
        a_re, a_im = both[:quarter, width:], both[quarter:, width:]
        h_re, h_im = spec_ref[j, :quarter, columns], spec_ref[j, quarter:, columns]
        for number, (real, imag) in enumerate(
            (
                (p_re * h_re - p_im * h_im, p_re * h_im + p_im * h_re),
                (h_re * a_re + h_im * a_im, h_re * a_im - h_im * a_re),
                (p_re * a_re + p_im * a_im, p_re * a_im - p_im * a_re),
            )
        ):
            into = slice(number * width, (number + 1) * width)
            mixed[j, :quarter, into] = real.astype(jnp.bfloat16)
            mixed[j, quarter:, into] = imag.astype(jnp.bfloat16)
        back[j] = jnp.dot(inv_ref[j], mixed[j], preferred_element_type=jnp.float32)

    @pl.loop(0, quarter // TILE)
    def _(step):
        begin = pl.multiple_of(step * TILE, TILE)
        real, imag = pl.ds(begin, TILE), pl.ds(begin + quarter, TILE)
        results = []
        for number in range(3):
            part = slice(number * width, (number + 1) * width)
            results.append(joined(*((back[j, real, part], back[j, imag, part]) for j in range(4))))
        for j, (combined, backward, filt) in enumerate(zip(*results)):
            here = pl.ds(begin + j * quarter, TILE)
            filt_rows[here, :] = filt * (1.0 / math.sqrt(rows))
            pltpu.make_async_copy(
                filt_rows.at[here, :], filt_ref.at[here, columns], filt_sem
            ).start()
            grads = (
                low(upstream[here, :] * combined),
                low(backward * value_rows[here, :]),
                low(backward * key_rows[here, :]),
            )
            for i in range(3):
                shifted_rows[i, here, :] = sum(taps[3 * s + i] * grads[s] for s in range(3))

    shifted_rows[:, rows:, :] = jnp.zeros((3, PAD, width), jnp.float32)

    @pl.loop(0, rows // LAST_TILE)
    def _(step):
        begin = pl.multiple_of(step * LAST_TILE, LAST_TILE)
        windows = [shifted_rows[i, pl.ds(begin, LAST_TILE + PAD), :] for i in range(3)]
        total = sum(windows[i][i : i + LAST_TILE, :] for i in range(3))
        grad_rows[pl.ds(begin, LAST_TILE), :] = total.astype(jnp.bfloat16)

    for k in range(devices):
        out_ref[k] = grad_rows[place(k if whole_out else me ^ k, 0), :]
    pltpu.make_async_copy(filt_rows, filt_ref.at[:, columns], filt_sem).wait()


def section(pieces, taps, fwd, inv, spec, chunk, filt, devices, whole_in, whole_out):
    length, width = pieces[0].shape[-2:]
    rows = devices * length
    near = pl.BlockSpec(memory_space=pltpu.VMEM)
    far = pl.BlockSpec(memory_space=pl.ANY)
    more = [] if filt is None else [filt]
    vmem = lambda *shape: pltpu.VMEM(shape, jnp.float32)
    return pl.pallas_call(
        functools.partial(section_kernel, devices, chunk, len(more), whole_in, whole_out),
        in_specs=[near] * len(pieces) + [far] + [near] * 3 + [far] * len(more),
        out_specs=[near, far],
        out_shape=[
            jax.ShapeDtypeStruct((devices, length, width), jnp.bfloat16),
            jax.ShapeDtypeStruct((rows, spec.shape[2]), jnp.float32),
        ],
        scratch_shapes=[
            vmem(rows + PAD, width),
            vmem(rows, width),
            vmem(rows, width),
            vmem(rows, width),
            pltpu.VMEM((4, rows // 2, 2 * width), jnp.bfloat16),
            pltpu.VMEM((4, rows // 2, 3 * width), jnp.bfloat16),
            vmem(4, rows // 2, 3 * width),
            vmem(3, rows + PAD, width),
            vmem(rows, width),
            pltpu.VMEM((rows, width), jnp.bfloat16),
            vmem(*taps.shape[1:3], width),
            pltpu.SemaphoreType.DMA,
            pltpu.SemaphoreType.DMA,
        ],
        input_output_aliases={len(pieces) + 4: 1} if more else {},
        compiler_params=pltpu.CompilerParams(vmem_limit_bytes=SECTION_VMEM),
        cost_estimate=pl.CostEstimate(
            flops=10 * rows * rows * width, bytes_accessed=30 * rows * width, transcendentals=0
        ),
        name="section",
    )(*pieces, taps, fwd, inv, spec, *more)


def phase_table(row_count, col_count, modulus, direction):
    row_ids = lax.broadcasted_iota(jnp.int32, (row_count, col_count), 0)
    col_ids = lax.broadcasted_iota(jnp.int32, (row_count, col_count), 1)
    residue = row_ids * col_ids % modulus
    angles = direction * 2.0 * math.pi / modulus * residue.astype(jnp.float32)
    return (jnp.cos(angles), jnp.sin(angles))


def highest(pattern, first_op, second_op):
    return jnp.einsum(pattern, first_op, second_op, precision=lax.Precision.HIGHEST)


def forward_spectrum(signal, half_q, width_p):
    full_q = 2 * half_q
    blocks = signal.reshape(half_q, width_p, signal.shape[1])
    fq_re, fq_im = phase_table(full_q, half_q, full_q, -1.0)
    section_re = highest("kq,qpc->kpc", fq_re, blocks)
    section_im = highest("kq,qpc->kpc", fq_im, blocks)
    tw_re, tw_im = phase_table(full_q, width_p, full_q * width_p, -1.0)
    turned_re = section_re * tw_re[:, :, None] - section_im * tw_im[:, :, None]
    turned_im = section_re * tw_im[:, :, None] + section_im * tw_re[:, :, None]
    fp_re, fp_im = phase_table(width_p, width_p, width_p, -1.0)
    out_re = highest("jp,kpc->jkc", fp_re, turned_re) - highest("jp,kpc->jkc", fp_im, turned_im)
    out_im = highest("jp,kpc->jkc", fp_re, turned_im) + highest("jp,kpc->jkc", fp_im, turned_re)
    return (out_re, out_im)


def inverse_field(spec_re, spec_im, half_q, width_p):
    full_q = 2 * half_q
    gp_re, gp_im = phase_table(width_p, width_p, width_p, 1.0)
    section_re = highest("mn,nqc->mqc", gp_re, spec_re) - highest("mn,nqc->mqc", gp_im, spec_im)
    section_im = highest("mn,nqc->mqc", gp_re, spec_im) + highest("mn,nqc->mqc", gp_im, spec_re)
    tw_re, tw_im = phase_table(width_p, full_q, full_q * width_p, 1.0)
    turned_re = section_re * tw_re[:, :, None] - section_im * tw_im[:, :, None]
    turned_im = section_re * tw_im[:, :, None] + section_im * tw_re[:, :, None]
    gq_re, gq_im = phase_table(half_q, full_q, full_q, 1.0)
    result = highest("aq,mqc->amc", gq_re, turned_re) - highest("aq,mqc->amc", gq_im, turned_im)
    return result.reshape(half_q * width_p, spec_re.shape[2]) / (full_q * width_p)


def large_section(x, g, taps, kernel, half_q):
    rows = x.shape[0]
    width_p = rows // half_q
    signal, upstream = x.astype(jnp.float32), g.astype(jnp.float32)
    moved = [jnp.pad(signal, ((i, 0), (0, 0)))[:rows] for i in range(3)]
    query, key, value = (
        sum(taps[3 * s + i] * moved[i] for i in range(3)).astype(jnp.bfloat16).astype(jnp.float32)
        for s in range(3)
    )
    p_re, p_im = forward_spectrum(key * value, half_q, width_p)
    a_re, a_im = forward_spectrum(upstream * query, half_q, width_p)
    h_re, h_im = forward_spectrum(kernel, half_q, width_p)
    combined = inverse_field(
        p_re * h_re - p_im * h_im, p_re * h_im + p_im * h_re, half_q, width_p
    )
    backward = inverse_field(
        h_re * a_re + h_im * a_im, h_re * a_im - h_im * a_re, half_q, width_p
    )
    filter_grad = inverse_field(
        p_re * a_re + p_im * a_im, p_re * a_im - p_im * a_re, half_q, width_p
    )
    grads = (upstream * combined, backward * value, backward * key)
    total = jnp.zeros_like(signal)
    for s in range(3):
        grad = grads[s].astype(jnp.bfloat16).astype(jnp.float32)
        for i in range(3):
            total = total + taps[3 * s + i] * jnp.pad(grad, ((0, i), (0, 0)))[i:]
    return total.astype(jnp.bfloat16), filter_grad * (1.0 / math.sqrt(rows))


def exchanged(chunk, devices, whole):
    if whole:
        return [lax.all_to_all(chunk[0], "seq", split_axis=0, concat_axis=0, tiled=True)]
    pairs = lambda k: [(i, i ^ k) for i in range(devices)]
    return [chunk[0]] + [lax.ppermute(chunk[k], "seq", pairs(k)) for k in range(1, devices)]


def fast(inputs, upstream, kernel, taps):
    devices, count = lax.axis_size("seq"), lax.axis_size("pipe")
    before = [(p, (p - 1) % count) for p in range(count)]
    arrived = [
        exchanged(chunk, devices, whole)
        for chunk, whole in zip(pack(inputs, upstream, devices, WHOLE_IN), WHOLE_IN)
    ]
    fwd, inv = quarter_tables(kernel.shape[0])
    spec = spectrum(kernel, fwd)
    filter_grad, home = None, []
    for chunk in range(CHUNKS):
        whole = WHOLE_OUT[chunk]
        grad, filter_grad = section(
            arrived[chunk], taps, fwd, inv, spec, chunk, filter_grad,
            devices, WHOLE_IN[chunk], whole,
        )
        grad = lax.ppermute(grad, "pipe", before)
        home.append(
            exchanged([grad] if whole else [grad[k] for k in range(devices)], devices, whole)
        )
    return unpack(home, devices, WHOLE_OUT), filter_grad[None]


def general(inputs, upstream, kernel, taps):
    devices, count = lax.axis_size("seq"), lax.axis_size("pipe")
    length_dev, model = inputs.shape
    rows, width = kernel.shape
    to_columns = lambda block: block.reshape(length_dev, devices, width).transpose(1, 0, 2)
    sent = jnp.stack([to_columns(inputs), to_columns(upstream)], axis=1)
    got = lax.all_to_all(sent, "seq", split_axis=0, concat_axis=0, tiled=True)
    x_cols, g_cols = got[:, 0].reshape(rows, width), got[:, 1].reshape(rows, width)
    grad_cols, filter_grad = large_section(x_cols, g_cols, taps, kernel, devices)
    back = lax.all_to_all(
        grad_cols.reshape(devices, length_dev, width), "seq", split_axis=0, concat_axis=0, tiled=True
    )
    grad_input = back.transpose(1, 0, 2).reshape(length_dev, model)
    received = lax.ppermute(
        grad_input[None], "pipe", [((i + 1) % count, i) for i in range(count)]
    )
    return received, filter_grad[None]


def shards(section_input, out_grad, conv_filter, short_taps):
    inputs, upstream, kernel = section_input[0], out_grad[0], conv_filter[0]
    devices = lax.axis_size("seq")
    model = inputs.shape[1]
    rows, width = kernel.shape
    dense = (
        rows <= DENSE_ROWS
        and rows % 256 == 0
        and width % (CHUNKS * 128) == 0
        and devices & (devices - 1) == 0
    )
    if dense:
        return fast(inputs, upstream, kernel, short_taps)
    taps = lax.dynamic_slice_in_dim(
        short_taps[0].reshape(-1, model), lax.axis_index("seq") * width, width, axis=1
    )
    return general(inputs, upstream, kernel, taps)


def solution(mesh):
    return jax.shard_map(
        shards,
        mesh=mesh,
        in_specs=(
            P("pipe", "seq", None),
            P("pipe", "seq", None),
            P("pipe", None, "seq"),
            P("pipe", None, None, None),
        ),
        out_specs=(P("pipe", "seq", None), P("pipe", None, "seq")),
        check_vma=False,
    )
```

```python
import functools
import math

import jax
import jax.numpy as jnp
import numpy as np
from jax import lax
from jax.experimental import pallas as pl
from jax.experimental.pallas import tpu as pltpu
from jax.sharding import PartitionSpec as P

WHOLE_IN = (False, False)
WHOLE_OUT = (True, False)
CHUNKS = len(WHOLE_IN)
PAD = 8
TILE = 16
LAST_TILE = 64
DENSE_ROWS = 1024
SPECTRUM_VMEM = 12 * 1024 * 1024
FILTER_VMEM = 10 * 1024 * 1024
SECTION_VMEM = 21 * 1024 * 1024
COS = [math.cos(math.pi / 8 * j) for j in range(4)]
SIN = [math.sin(math.pi / 8 * j) for j in range(4)]


def quarter_tables(rows):
    quarter = rows // 4
    freqs = 16 * np.arange(quarter)[None, :, None] + 4 * np.arange(4)[:, None, None] + 1
    angles = 2.0 * np.pi / (4 * rows) * (freqs * np.arange(quarter) % (4 * rows))
    real, imag = np.cos(angles), -np.sin(angles)
    fwd = np.concatenate(
        [np.concatenate([real, -imag], axis=2), np.concatenate([imag, real], axis=2)], axis=1
    )
    inv = np.swapaxes(fwd, 1, 2) / rows
    return jnp.asarray(fwd.astype(jnp.bfloat16)), jnp.asarray(inv.astype(jnp.bfloat16))


def split(x0, x1, x2, x3):
    even, turn = x0 + COS[2] * x2, SIN[2] * x2
    odd = x0 - COS[2] * x2
    sum_re, sum_im = COS[1] * x1 + COS[3] * x3, SIN[1] * x1 + SIN[3] * x3
    dif_re, dif_im = COS[1] * x1 - COS[3] * x3, SIN[1] * x1 - SIN[3] * x3
    return (
        (even + sum_re, -turn - sum_im),
        (odd - dif_im, turn - dif_re),
        (even - sum_re, sum_im - turn),
        (odd + dif_im, turn + dif_re),
    )


def joined(v0, v1, v2, v3):
    a_re, a_im, b_re, b_im = v0[0] + v2[0], v0[1] + v2[1], v1[0] + v3[0], v1[1] + v3[1]
    c_re, c_im, d_re, d_im = v0[0] - v2[0], v0[1] - v2[1], v1[0] - v3[0], v1[1] - v3[1]
    return (
        a_re + b_re,
        COS[1] * (c_re - d_im) - SIN[1] * (c_im + d_re),
        COS[2] * (a_re - b_re) - SIN[2] * (a_im - b_im),
        COS[3] * (c_re + d_im) - SIN[3] * (c_im - d_re),
    )


def by_target(refs, devices, whole):
    me, refs = lax.axis_index("seq"), list(refs)
    pairs = []
    for together in whole:
        if together:
            ref = refs.pop(0)
            pairs.append([(d, ref.at[d]) for d in range(devices)])
        else:
            pairs.append([(me ^ k, refs.pop(0)) for k in range(devices)])
    return pairs


def pack_kernel(whole, x_ref, g_ref, *refs):
    pieces, sem = refs[:-1], refs[-1]
    devices = lax.axis_size("seq")
    width = pieces[0].shape[-1]
    copies = []
    for chunk, pairs in enumerate(by_target(pieces, devices, whole)):
        for number, (device, piece) in enumerate(pairs):
            start = pl.multiple_of((device * len(whole) + chunk) * width, width)
            for half, ref in enumerate((x_ref, g_ref)):
                copies.append(
                    pltpu.make_async_copy(
                        ref.at[:, pl.ds(start, width)],
                        piece.at[half],
                        sem.at[chunk * devices + number, half],
                    )
                )
    for copy in copies:
        copy.start()
    for copy in copies:
        copy.wait()


def pack(x, g, devices, whole):
    length, model = x.shape
    width = model // devices // len(whole)
    shapes = []
    for together in whole:
        shapes += [(devices, 2, length, width)] if together else [(2, length, width)] * devices
    pieces = pl.pallas_call(
        functools.partial(pack_kernel, whole),
        in_specs=[pl.BlockSpec(memory_space=pl.ANY)] * 2,
        out_specs=[pl.BlockSpec(memory_space=pltpu.VMEM)] * len(shapes),
        out_shape=[jax.ShapeDtypeStruct(shape, x.dtype) for shape in shapes],
        scratch_shapes=[pltpu.SemaphoreType.DMA((devices * len(whole), 2))],
        compiler_params=pltpu.CompilerParams(vmem_limit_bytes=8 * 1024 * 1024),
        name="pack",
    )(x, g)
    chunks, pieces = [], list(pieces)
    for together in whole:
        taken = 1 if together else devices
        chunks.append(pieces[:taken])
        pieces = pieces[taken:]
    return chunks


def unpack_kernel(whole, *refs):
    pieces, out_ref, sem = refs[:-2], refs[-2], refs[-1]
    devices = lax.axis_size("seq")
    width = pieces[0].shape[-1]
    copies = []
    for chunk, pairs in enumerate(by_target(pieces, devices, whole)):
        for number, (device, piece) in enumerate(pairs):
            start = pl.multiple_of((device * len(whole) + chunk) * width, width)
            copies.append(
                pltpu.make_async_copy(
                    piece,
                    out_ref.at[0, :, pl.ds(start, width)],
                    sem.at[chunk * devices + number],
                )
            )
    for copy in copies:
        copy.start()
    for copy in copies:
        copy.wait()


def unpack(chunks, devices, whole):
    flat = [piece for chunk in chunks for piece in chunk]
    length, width = flat[0].shape[-2:]
    count = devices * len(whole)
    return pl.pallas_call(
        functools.partial(unpack_kernel, whole),
        in_specs=[pl.BlockSpec(memory_space=pltpu.VMEM)] * len(flat),
        out_specs=pl.BlockSpec(memory_space=pl.ANY),
        out_shape=jax.ShapeDtypeStruct((1, length, width * count), flat[0].dtype),
        scratch_shapes=[pltpu.SemaphoreType.DMA((count,))],
        compiler_params=pltpu.CompilerParams(vmem_limit_bytes=8 * 1024 * 1024),
        name="unpack",
    )(*flat)


def spectrum_kernel(kernel_ref, fwd_ref, spec_ref, turned):
    rows = kernel_ref.shape[0]
    quarter = rows // 4

    @pl.loop(0, quarter // TILE)
    def _(step):
        start = pl.multiple_of(step * TILE, TILE)
        parts = split(*(kernel_ref[pl.ds(start + j * quarter, TILE), :] for j in range(4)))
        for j, (real, imag) in enumerate(parts):
            turned[j, pl.ds(start, TILE), :] = real.astype(jnp.bfloat16)
            turned[j, pl.ds(start + quarter, TILE), :] = imag.astype(jnp.bfloat16)

    for j in range(4):
        spec_ref[j] = jnp.dot(fwd_ref[j], turned[j], preferred_element_type=jnp.float32)


def spectrum(kernel, fwd):
    rows, width = kernel.shape
    near = pl.BlockSpec(memory_space=pltpu.VMEM)
    return pl.pallas_call(
        spectrum_kernel,
        in_specs=[near] * 2,
        out_specs=near,
        out_shape=jax.ShapeDtypeStruct((4, rows // 2, width), jnp.float32),
        scratch_shapes=[pltpu.VMEM((4, rows // 2, width), jnp.bfloat16)],
        compiler_params=pltpu.CompilerParams(vmem_limit_bytes=SPECTRUM_VMEM),
        cost_estimate=pl.CostEstimate(
            flops=2 * rows * rows * width, bytes_accessed=14 * rows * width, transcendentals=0
        ),
        name="spectrum",
    )(kernel, fwd)


def section_kernel(devices, chunk, whole_in, whole_out, *refs):
    taken = 1 if whole_in else devices
    (pieces,) = by_target(refs[:taken], devices, [whole_in])
    tap_ref, spec_ref, fwd_ref, inv_ref, out_ref, cross_ref = refs[taken : taken + 6]
    padded, upstream, key_rows, value_rows, turned, mixed, back = refs[taken + 6 : taken + 13]
    shifted_rows, grad_rows, tap_rows, tap_sem = refs[taken + 13 :]
    me = lax.axis_index("seq")
    length, width = pieces[0][1].shape[1:]
    rows = length * devices
    quarter = rows // 4
    columns = slice(chunk * width, (chunk + 1) * width)
    place = lambda device, offset: pl.ds(pl.multiple_of(device * length + offset, 8), length)
    low = lambda v: v.astype(jnp.bfloat16).astype(jnp.float32)

    start = pl.multiple_of((me * (spec_ref.shape[2] // width) + chunk) * width, width)
    fetch = pltpu.make_async_copy(tap_ref.at[0, :, :, pl.ds(start, width)], tap_rows, tap_sem)
    fetch.start()
    padded[0:PAD, :] = jnp.zeros((PAD, width), jnp.float32)
    for device, piece in pieces:
        padded[place(device, PAD), :] = piece[0].astype(jnp.float32)
        upstream[place(device, 0), :] = piece[1].astype(jnp.float32)
    fetch.wait()
    taps = [tap_rows[s, i : i + 1, :] for s in range(3) for i in range(3)]

    @pl.loop(0, quarter // TILE)
    def _(step):
        begin = pl.multiple_of(step * TILE, TILE)
        products, adjoints = [], []
        for j in range(4):
            here = pl.ds(begin + j * quarter, TILE)
            window = padded[pl.ds(begin + j * quarter, TILE + PAD), :]
            moved = [window[PAD - i : PAD - i + TILE, :] for i in range(3)]
            query, key, value = (
                low(sum(taps[3 * s + i] * moved[i] for i in range(3))) for s in range(3)
            )
            key_rows[here, :] = key
            value_rows[here, :] = value
            products.append(key * value)
            adjoints.append(upstream[here, :] * query)
        for number, signals in enumerate((products, adjoints)):
            into = slice(number * width, (number + 1) * width)
            for j, (real, imag) in enumerate(split(*signals)):
                turned[j, pl.ds(begin, TILE), into] = real.astype(jnp.bfloat16)
                turned[j, pl.ds(begin + quarter, TILE), into] = imag.astype(jnp.bfloat16)

    for j in range(4):
        both = jnp.dot(fwd_ref[j], turned[j], preferred_element_type=jnp.float32)
        p_re, p_im = both[:quarter, :width], both[quarter:, :width]
        a_re, a_im = both[:quarter, width:], both[quarter:, width:]
        h_re, h_im = spec_ref[j, :quarter, columns], spec_ref[j, quarter:, columns]
        mixed[j, :quarter, :width] = (p_re * h_re - p_im * h_im).astype(jnp.bfloat16)
        mixed[j, quarter:, :width] = (p_re * h_im + p_im * h_re).astype(jnp.bfloat16)
        mixed[j, :quarter, width:] = (h_re * a_re + h_im * a_im).astype(jnp.bfloat16)
        mixed[j, quarter:, width:] = (h_re * a_im - h_im * a_re).astype(jnp.bfloat16)
        cross_ref[j, :quarter, :] = (p_re * a_re + p_im * a_im).astype(jnp.bfloat16)
        cross_ref[j, quarter:, :] = (p_re * a_im - p_im * a_re).astype(jnp.bfloat16)
        back[j] = jnp.dot(inv_ref[j], mixed[j], preferred_element_type=jnp.float32)

    @pl.loop(0, quarter // TILE)
    def _(step):
        begin = pl.multiple_of(step * TILE, TILE)
        real, imag = pl.ds(begin, TILE), pl.ds(begin + quarter, TILE)
        results = []
        for part in (slice(0, width), slice(width, 2 * width)):
            results.append(joined(*((back[j, real, part], back[j, imag, part]) for j in range(4))))
        for j, (combined, backward) in enumerate(zip(*results)):
            here = pl.ds(begin + j * quarter, TILE)
            grads = (
                low(upstream[here, :] * combined),
                low(backward * value_rows[here, :]),
                low(backward * key_rows[here, :]),
            )
            for i in range(3):
                shifted_rows[i, here, :] = sum(taps[3 * s + i] * grads[s] for s in range(3))

    shifted_rows[:, rows:, :] = jnp.zeros((3, PAD, width), jnp.float32)

    @pl.loop(0, rows // LAST_TILE)
    def _(step):
        begin = pl.multiple_of(step * LAST_TILE, LAST_TILE)
        windows = [shifted_rows[i, pl.ds(begin, LAST_TILE + PAD), :] for i in range(3)]
        total = sum(windows[i][i : i + LAST_TILE, :] for i in range(3))
        grad_rows[pl.ds(begin, LAST_TILE), :] = total.astype(jnp.bfloat16)

    for k in range(devices):
        out_ref[k] = grad_rows[place(k if whole_out else me ^ k, 0), :]


def section(pieces, taps, spec, fwd, inv, chunk, devices, whole_in, whole_out):
    length, width = pieces[0].shape[-2:]
    rows = devices * length
    near = pl.BlockSpec(memory_space=pltpu.VMEM)
    far = pl.BlockSpec(memory_space=pl.ANY)
    single = lambda *shape: pltpu.VMEM(shape, jnp.float32)
    half = lambda *shape: pltpu.VMEM(shape, jnp.bfloat16)
    return pl.pallas_call(
        functools.partial(section_kernel, devices, chunk, whole_in, whole_out),
        in_specs=[near] * len(pieces) + [far] + [near] * 3,
        out_specs=[near] * 2,
        out_shape=[
            jax.ShapeDtypeStruct((devices, length, width), jnp.bfloat16),
            jax.ShapeDtypeStruct((4, rows // 2, width), jnp.bfloat16),
        ],
        scratch_shapes=[
            single(rows + PAD, width),
            single(rows, width),
            single(rows, width),
            single(rows, width),
            half(4, rows // 2, 2 * width),
            half(4, rows // 2, 2 * width),
            single(4, rows // 2, 2 * width),
            single(3, rows + PAD, width),
            half(rows, width),
            single(*taps.shape[1:3], width),
            pltpu.SemaphoreType.DMA,
        ],
        compiler_params=pltpu.CompilerParams(vmem_limit_bytes=SECTION_VMEM),
        cost_estimate=pl.CostEstimate(
            flops=10 * rows * rows * width, bytes_accessed=20 * rows * width, transcendentals=0
        ),
        name="section",
    )(*pieces, taps, spec, fwd, inv)


def filter_kernel(inv_ref, *refs):
    crosses, (filt_ref, back, filt_rows, sem) = refs[:-4], refs[-4:]
    rows, width = filt_rows.shape[1:]
    quarter = rows // 4
    for chunk, cross_ref in enumerate(crosses):
        columns = slice(chunk * width, (chunk + 1) * width)
        for j in range(4):
            back[chunk, j] = jnp.dot(inv_ref[j], cross_ref[j], preferred_element_type=jnp.float32)

        @pl.loop(0, quarter // TILE)
        def _(step):
            begin = pl.multiple_of(step * TILE, TILE)
            real, imag = pl.ds(begin, TILE), pl.ds(begin + quarter, TILE)
            parts = joined(*((back[chunk, j, real, :], back[chunk, j, imag, :]) for j in range(4)))
            for j, part in enumerate(parts):
                filt_rows[chunk, pl.ds(begin + j * quarter, TILE), :] = part * (1.0 / math.sqrt(rows))

        pltpu.make_async_copy(filt_rows.at[chunk], filt_ref.at[:, columns], sem.at[chunk]).start()
    for chunk in range(len(crosses)):
        columns = slice(chunk * width, (chunk + 1) * width)
        pltpu.make_async_copy(filt_rows.at[chunk], filt_ref.at[:, columns], sem.at[chunk]).wait()


def filter_gradient(inv, crosses):
    rows, width = 2 * crosses[0].shape[1], crosses[0].shape[2]
    count = len(crosses)
    return pl.pallas_call(
        filter_kernel,
        in_specs=[pl.BlockSpec(memory_space=pltpu.VMEM)] * (1 + count),
        out_specs=pl.BlockSpec(memory_space=pl.ANY),
        out_shape=jax.ShapeDtypeStruct((rows, width * count), jnp.float32),
        scratch_shapes=[
            pltpu.VMEM((count, 4, rows // 2, width), jnp.float32),
            pltpu.VMEM((count, rows, width), jnp.float32),
            pltpu.SemaphoreType.DMA((count,)),
        ],
        compiler_params=pltpu.CompilerParams(vmem_limit_bytes=FILTER_VMEM),
        cost_estimate=pl.CostEstimate(
            flops=2 * rows * rows * width * count,
            bytes_accessed=6 * rows * width * count,
            transcendentals=0,
        ),
        name="filter",
    )(inv, *crosses)


def phase_table(row_count, col_count, modulus, direction):
    row_ids = lax.broadcasted_iota(jnp.int32, (row_count, col_count), 0)
    col_ids = lax.broadcasted_iota(jnp.int32, (row_count, col_count), 1)
    residue = row_ids * col_ids % modulus
    angles = direction * 2.0 * math.pi / modulus * residue.astype(jnp.float32)
    return (jnp.cos(angles), jnp.sin(angles))


def highest(pattern, first_op, second_op):
    return jnp.einsum(pattern, first_op, second_op, precision=lax.Precision.HIGHEST)


def forward_spectrum(signal, half_q, width_p):
    full_q = 2 * half_q
    blocks = signal.reshape(half_q, width_p, signal.shape[1])
    fq_re, fq_im = phase_table(full_q, half_q, full_q, -1.0)
    section_re = highest("kq,qpc->kpc", fq_re, blocks)
    section_im = highest("kq,qpc->kpc", fq_im, blocks)
    tw_re, tw_im = phase_table(full_q, width_p, full_q * width_p, -1.0)
    turned_re = section_re * tw_re[:, :, None] - section_im * tw_im[:, :, None]
    turned_im = section_re * tw_im[:, :, None] + section_im * tw_re[:, :, None]
    fp_re, fp_im = phase_table(width_p, width_p, width_p, -1.0)
    out_re = highest("jp,kpc->jkc", fp_re, turned_re) - highest("jp,kpc->jkc", fp_im, turned_im)
    out_im = highest("jp,kpc->jkc", fp_re, turned_im) + highest("jp,kpc->jkc", fp_im, turned_re)
    return (out_re, out_im)


def inverse_field(spec_re, spec_im, half_q, width_p):
    full_q = 2 * half_q
    gp_re, gp_im = phase_table(width_p, width_p, width_p, 1.0)
    section_re = highest("mn,nqc->mqc", gp_re, spec_re) - highest("mn,nqc->mqc", gp_im, spec_im)
    section_im = highest("mn,nqc->mqc", gp_re, spec_im) + highest("mn,nqc->mqc", gp_im, spec_re)
    tw_re, tw_im = phase_table(width_p, full_q, full_q * width_p, 1.0)
    turned_re = section_re * tw_re[:, :, None] - section_im * tw_im[:, :, None]
    turned_im = section_re * tw_im[:, :, None] + section_im * tw_re[:, :, None]
    gq_re, gq_im = phase_table(half_q, full_q, full_q, 1.0)
    result = highest("aq,mqc->amc", gq_re, turned_re) - highest("aq,mqc->amc", gq_im, turned_im)
    return result.reshape(half_q * width_p, spec_re.shape[2]) / (full_q * width_p)


def large_section(x, g, taps, kernel, half_q):
    rows = x.shape[0]
    width_p = rows // half_q
    signal, upstream = x.astype(jnp.float32), g.astype(jnp.float32)
    moved = [jnp.pad(signal, ((i, 0), (0, 0)))[:rows] for i in range(3)]
    query, key, value = (
        sum(taps[3 * s + i] * moved[i] for i in range(3)).astype(jnp.bfloat16).astype(jnp.float32)
        for s in range(3)
    )
    p_re, p_im = forward_spectrum(key * value, half_q, width_p)
    a_re, a_im = forward_spectrum(upstream * query, half_q, width_p)
    h_re, h_im = forward_spectrum(kernel, half_q, width_p)
    combined = inverse_field(
        p_re * h_re - p_im * h_im, p_re * h_im + p_im * h_re, half_q, width_p
    )
    backward = inverse_field(
        h_re * a_re + h_im * a_im, h_re * a_im - h_im * a_re, half_q, width_p
    )
    filter_grad = inverse_field(
        p_re * a_re + p_im * a_im, p_re * a_im - p_im * a_re, half_q, width_p
    )
    grads = (upstream * combined, backward * value, backward * key)
    total = jnp.zeros_like(signal)
    for s in range(3):
        grad = grads[s].astype(jnp.bfloat16).astype(jnp.float32)
        for i in range(3):
            total = total + taps[3 * s + i] * jnp.pad(grad, ((0, i), (0, 0)))[i:]
    return total.astype(jnp.bfloat16), filter_grad * (1.0 / math.sqrt(rows))


def exchanged(chunk, devices, whole):
    if whole:
        return [lax.all_to_all(chunk[0], "seq", split_axis=0, concat_axis=0, tiled=True)]
    pairs = lambda k: [(i, i ^ k) for i in range(devices)]
    return [chunk[0]] + [lax.ppermute(chunk[k], "seq", pairs(k)) for k in range(1, devices)]


def fast(inputs, upstream, kernel, taps):
    devices, count = lax.axis_size("seq"), lax.axis_size("pipe")
    before = [(p, (p - 1) % count) for p in range(count)]
    pieces = pack(inputs, upstream, devices, WHOLE_IN)
    fwd, inv = quarter_tables(kernel.shape[0])
    spec = spectrum(kernel, fwd)
    grads, crosses = [], []
    for chunk in range(CHUNKS):
        arrived = exchanged(pieces[chunk], devices, WHOLE_IN[chunk])
        grad, cross = section(
            arrived, taps, spec, fwd, inv, chunk, devices, WHOLE_IN[chunk], WHOLE_OUT[chunk]
        )
        grads.append(lax.ppermute(grad, "pipe", before))
        crosses.append(cross)
    filter_grad = filter_gradient(inv, crosses)
    home = []
    for grad, whole in zip(grads, WHOLE_OUT):
        grad, filter_grad = lax.optimization_barrier((grad, filter_grad))
        home.append(
            exchanged([grad] if whole else [grad[k] for k in range(devices)], devices, whole)
        )
    return unpack(home, devices, WHOLE_OUT), filter_grad[None]


def general(inputs, upstream, kernel, taps):
    devices, count = lax.axis_size("seq"), lax.axis_size("pipe")
    length_dev, model = inputs.shape
    rows, width = kernel.shape
    to_columns = lambda block: block.reshape(length_dev, devices, width).transpose(1, 0, 2)
    sent = jnp.stack([to_columns(inputs), to_columns(upstream)], axis=1)
    got = lax.all_to_all(sent, "seq", split_axis=0, concat_axis=0, tiled=True)
    x_cols, g_cols = got[:, 0].reshape(rows, width), got[:, 1].reshape(rows, width)
    grad_cols, filter_grad = large_section(x_cols, g_cols, taps, kernel, devices)
    back = lax.all_to_all(
        grad_cols.reshape(devices, length_dev, width), "seq", split_axis=0, concat_axis=0, tiled=True
    )
    grad_input = back.transpose(1, 0, 2).reshape(length_dev, model)
    received = lax.ppermute(
        grad_input[None], "pipe", [((i + 1) % count, i) for i in range(count)]
    )
    return received, filter_grad[None]


def shards(section_input, out_grad, conv_filter, short_taps):
    inputs, upstream, kernel = section_input[0], out_grad[0], conv_filter[0]
    devices = lax.axis_size("seq")
    model = inputs.shape[1]
    rows, width = kernel.shape
    dense = (
        rows <= DENSE_ROWS
        and rows % 256 == 0
        and width % (CHUNKS * 128) == 0
        and devices & (devices - 1) == 0
    )
    if dense:
        return fast(inputs, upstream, kernel, short_taps)
    taps = lax.dynamic_slice_in_dim(
        short_taps[0].reshape(-1, model), lax.axis_index("seq") * width, width, axis=1
    )
    return general(inputs, upstream, kernel, taps)


def solution(mesh):
    return jax.shard_map(
        shards,
        mesh=mesh,
        in_specs=(
            P("pipe", "seq", None),
            P("pipe", "seq", None),
            P("pipe", None, "seq"),
            P("pipe", None, None, None),
        ),
        out_specs=(P("pipe", "seq", None), P("pipe", None, "seq")),
        check_vma=False,
    )
```

```python
import functools
import math

import jax
import jax.numpy as jnp
import numpy as np
from jax import lax
from jax.experimental import pallas as pl
from jax.experimental.pallas import tpu as pltpu
from jax.sharding import PartitionSpec as P

WHOLE_IN = (False, False)
WHOLE_OUT = (True, False)
PARTS = (1, 2)
CHUNKS = len(WHOLE_IN)
PAD = 8
TILE = 16
LAST_TILE = 64
DENSE_ROWS = 1024
SPECTRUM_VMEM = 12 * 1024 * 1024
FILTER_VMEM = 10 * 1024 * 1024
SECTION_VMEM = 21 * 1024 * 1024
COS = [math.cos(math.pi / 8 * j) for j in range(4)]
SIN = [math.sin(math.pi / 8 * j) for j in range(4)]


def quarter_tables(rows):
    quarter = rows // 4
    freqs = 16 * np.arange(quarter)[None, :, None] + 4 * np.arange(4)[:, None, None] + 1
    angles = 2.0 * np.pi / (4 * rows) * (freqs * np.arange(quarter) % (4 * rows))
    real, imag = np.cos(angles), -np.sin(angles)
    fwd = np.concatenate(
        [np.concatenate([real, -imag], axis=2), np.concatenate([imag, real], axis=2)], axis=1
    )
    inv = np.swapaxes(fwd, 1, 2) / rows
    return jnp.asarray(fwd.astype(jnp.bfloat16)), jnp.asarray(inv.astype(jnp.bfloat16))


def split(x0, x1, x2, x3):
    even, turn = x0 + COS[2] * x2, SIN[2] * x2
    odd = x0 - COS[2] * x2
    sum_re, sum_im = COS[1] * x1 + COS[3] * x3, SIN[1] * x1 + SIN[3] * x3
    dif_re, dif_im = COS[1] * x1 - COS[3] * x3, SIN[1] * x1 - SIN[3] * x3
    return (
        (even + sum_re, -turn - sum_im),
        (odd - dif_im, turn - dif_re),
        (even - sum_re, sum_im - turn),
        (odd + dif_im, turn + dif_re),
    )


def joined(v0, v1, v2, v3):
    a_re, a_im, b_re, b_im = v0[0] + v2[0], v0[1] + v2[1], v1[0] + v3[0], v1[1] + v3[1]
    c_re, c_im, d_re, d_im = v0[0] - v2[0], v0[1] - v2[1], v1[0] - v3[0], v1[1] - v3[1]
    return (
        a_re + b_re,
        COS[1] * (c_re - d_im) - SIN[1] * (c_im + d_re),
        COS[2] * (a_re - b_re) - SIN[2] * (a_im - b_im),
        COS[3] * (c_re + d_im) - SIN[3] * (c_im - d_re),
    )


def by_target(refs, devices, whole):
    me, refs = lax.axis_index("seq"), list(refs)
    pairs = []
    for together in whole:
        if together:
            ref = refs.pop(0)
            pairs.append([(d, ref.at[d]) for d in range(devices)])
        else:
            pairs.append([(me ^ k, refs.pop(0)) for k in range(devices)])
    return pairs


def pack_kernel(whole, x_ref, g_ref, *refs):
    pieces, sem = refs[:-1], refs[-1]
    devices = lax.axis_size("seq")
    width = pieces[0].shape[-1]
    copies = []
    for chunk, pairs in enumerate(by_target(pieces, devices, whole)):
        for number, (device, piece) in enumerate(pairs):
            start = pl.multiple_of((device * len(whole) + chunk) * width, width)
            for half, ref in enumerate((x_ref, g_ref)):
                copies.append(
                    pltpu.make_async_copy(
                        ref.at[:, pl.ds(start, width)],
                        piece.at[half],
                        sem.at[chunk * devices + number, half],
                    )
                )
    for copy in copies:
        copy.start()
    for copy in copies:
        copy.wait()


def pack(x, g, devices, whole):
    length, model = x.shape
    width = model // devices // len(whole)
    shapes = []
    for together in whole:
        shapes += [(devices, 2, length, width)] if together else [(2, length, width)] * devices
    pieces = pl.pallas_call(
        functools.partial(pack_kernel, whole),
        in_specs=[pl.BlockSpec(memory_space=pl.ANY)] * 2,
        out_specs=[pl.BlockSpec(memory_space=pltpu.VMEM)] * len(shapes),
        out_shape=[jax.ShapeDtypeStruct(shape, x.dtype) for shape in shapes],
        scratch_shapes=[pltpu.SemaphoreType.DMA((devices * len(whole), 2))],
        compiler_params=pltpu.CompilerParams(vmem_limit_bytes=8 * 1024 * 1024),
        name="pack",
    )(x, g)
    chunks, pieces = [], list(pieces)
    for together in whole:
        taken = 1 if together else devices
        chunks.append(pieces[:taken])
        pieces = pieces[taken:]
    return chunks


def unpack_kernel(whole, *refs):
    pieces, out_ref, sem = refs[:-2], refs[-2], refs[-1]
    devices = lax.axis_size("seq")
    width = pieces[0].shape[-1]
    copies = []
    for chunk, pairs in enumerate(by_target(pieces, devices, whole)):
        for number, (device, piece) in enumerate(pairs):
            start = pl.multiple_of((device * len(whole) + chunk) * width, width)
            copies.append(
                pltpu.make_async_copy(
                    piece,
                    out_ref.at[0, :, pl.ds(start, width)],
                    sem.at[chunk * devices + number],
                )
            )
    for copy in copies:
        copy.start()
    for copy in copies:
        copy.wait()


def unpack(chunks, devices, whole):
    flat = [piece for chunk in chunks for piece in chunk]
    length, width = flat[0].shape[-2:]
    count = devices * len(whole)
    return pl.pallas_call(
        functools.partial(unpack_kernel, whole),
        in_specs=[pl.BlockSpec(memory_space=pltpu.VMEM)] * len(flat),
        out_specs=pl.BlockSpec(memory_space=pl.ANY),
        out_shape=jax.ShapeDtypeStruct((1, length, width * count), flat[0].dtype),
        scratch_shapes=[pltpu.SemaphoreType.DMA((count,))],
        compiler_params=pltpu.CompilerParams(vmem_limit_bytes=8 * 1024 * 1024),
        name="unpack",
    )(*flat)


def spectrum_kernel(kernel_ref, fwd_ref, spec_ref, turned):
    rows = kernel_ref.shape[0]
    quarter = rows // 4

    @pl.loop(0, quarter // TILE)
    def _(step):
        start = pl.multiple_of(step * TILE, TILE)
        parts = split(*(kernel_ref[pl.ds(start + j * quarter, TILE), :] for j in range(4)))
        for j, (real, imag) in enumerate(parts):
            turned[j, pl.ds(start, TILE), :] = real.astype(jnp.bfloat16)
            turned[j, pl.ds(start + quarter, TILE), :] = imag.astype(jnp.bfloat16)

    for j in range(4):
        spec_ref[j] = jnp.dot(fwd_ref[j], turned[j], preferred_element_type=jnp.float32)


def spectrum(kernel, fwd):
    rows, width = kernel.shape
    near = pl.BlockSpec(memory_space=pltpu.VMEM)
    return pl.pallas_call(
        spectrum_kernel,
        in_specs=[near] * 2,
        out_specs=near,
        out_shape=jax.ShapeDtypeStruct((4, rows // 2, width), jnp.float32),
        scratch_shapes=[pltpu.VMEM((4, rows // 2, width), jnp.bfloat16)],
        compiler_params=pltpu.CompilerParams(vmem_limit_bytes=SPECTRUM_VMEM),
        cost_estimate=pl.CostEstimate(
            flops=2 * rows * rows * width, bytes_accessed=14 * rows * width, transcendentals=0
        ),
        name="spectrum",
    )(kernel, fwd)


def section_kernel(devices, chunk, whole_in, whole_out, parts, *refs):
    taken = 1 if whole_in else devices
    (pieces,) = by_target(refs[:taken], devices, [whole_in])
    tap_ref, spec_ref, fwd_ref, inv_ref = refs[taken : taken + 4]
    refs = refs[taken + 4 :]
    out_refs, refs = refs[:parts], refs[parts:]
    cross_ref, refs = refs[0], refs[1:]
    padded, upstream, key_rows, value_rows, turned, mixed, back = refs[:7]
    shifted_rows, grad_rows, tap_rows, tap_sem = refs[7:]
    me = lax.axis_index("seq")
    length, width = pieces[0][1].shape[1:]
    rows = length * devices
    quarter = rows // 4
    columns = slice(chunk * width, (chunk + 1) * width)
    place = lambda device, offset: pl.ds(pl.multiple_of(device * length + offset, 8), length)
    low = lambda v: v.astype(jnp.bfloat16).astype(jnp.float32)

    start = pl.multiple_of((me * (spec_ref.shape[2] // width) + chunk) * width, width)
    fetch = pltpu.make_async_copy(tap_ref.at[0, :, :, pl.ds(start, width)], tap_rows, tap_sem)
    fetch.start()
    padded[0:PAD, :] = jnp.zeros((PAD, width), jnp.float32)
    for device, piece in pieces:
        padded[place(device, PAD), :] = piece[0].astype(jnp.float32)
        upstream[place(device, 0), :] = piece[1].astype(jnp.float32)
    fetch.wait()
    taps = [tap_rows[s, i : i + 1, :] for s in range(3) for i in range(3)]

    @pl.loop(0, quarter // TILE)
    def _(step):
        begin = pl.multiple_of(step * TILE, TILE)
        products, adjoints = [], []
        for j in range(4):
            here = pl.ds(begin + j * quarter, TILE)
            window = padded[pl.ds(begin + j * quarter, TILE + PAD), :]
            moved = [window[PAD - i : PAD - i + TILE, :] for i in range(3)]
            query, key, value = (
                low(sum(taps[3 * s + i] * moved[i] for i in range(3))) for s in range(3)
            )
            key_rows[here, :] = key
            value_rows[here, :] = value
            products.append(key * value)
            adjoints.append(upstream[here, :] * query)
        for number, signals in enumerate((products, adjoints)):
            into = slice(number * width, (number + 1) * width)
            for j, (real, imag) in enumerate(split(*signals)):
                turned[j, pl.ds(begin, TILE), into] = real.astype(jnp.bfloat16)
                turned[j, pl.ds(begin + quarter, TILE), into] = imag.astype(jnp.bfloat16)

    for j in range(4):
        both = jnp.dot(fwd_ref[j], turned[j], preferred_element_type=jnp.float32)
        p_re, p_im = both[:quarter, :width], both[quarter:, :width]
        a_re, a_im = both[:quarter, width:], both[quarter:, width:]
        h_re, h_im = spec_ref[j, :quarter, columns], spec_ref[j, quarter:, columns]
        mixed[j, :quarter, :width] = (p_re * h_re - p_im * h_im).astype(jnp.bfloat16)
        mixed[j, quarter:, :width] = (p_re * h_im + p_im * h_re).astype(jnp.bfloat16)
        mixed[j, :quarter, width:] = (h_re * a_re + h_im * a_im).astype(jnp.bfloat16)
        mixed[j, quarter:, width:] = (h_re * a_im - h_im * a_re).astype(jnp.bfloat16)
        cross_ref[j, :quarter, :] = (p_re * a_re + p_im * a_im).astype(jnp.bfloat16)
        cross_ref[j, quarter:, :] = (p_re * a_im - p_im * a_re).astype(jnp.bfloat16)
        back[j] = jnp.dot(inv_ref[j], mixed[j], preferred_element_type=jnp.float32)

    @pl.loop(0, quarter // TILE)
    def _(step):
        begin = pl.multiple_of(step * TILE, TILE)
        real, imag = pl.ds(begin, TILE), pl.ds(begin + quarter, TILE)
        results = []
        for part in (slice(0, width), slice(width, 2 * width)):
            results.append(joined(*((back[j, real, part], back[j, imag, part]) for j in range(4))))
        for j, (combined, backward) in enumerate(zip(*results)):
            here = pl.ds(begin + j * quarter, TILE)
            grads = (
                low(upstream[here, :] * combined),
                low(backward * value_rows[here, :]),
                low(backward * key_rows[here, :]),
            )
            for i in range(3):
                shifted_rows[i, here, :] = sum(taps[3 * s + i] * grads[s] for s in range(3))

    shifted_rows[:, rows:, :] = jnp.zeros((3, PAD, width), jnp.float32)

    @pl.loop(0, rows // LAST_TILE)
    def _(step):
        begin = pl.multiple_of(step * LAST_TILE, LAST_TILE)
        windows = [shifted_rows[i, pl.ds(begin, LAST_TILE + PAD), :] for i in range(3)]
        total = sum(windows[i][i : i + LAST_TILE, :] for i in range(3))
        grad_rows[pl.ds(begin, LAST_TILE), :] = total.astype(jnp.bfloat16)

    for k in range(devices):
        number, within = divmod(k, devices // parts)
        out_refs[number][within] = grad_rows[place(k if whole_out else me ^ k, 0), :]


def section(pieces, taps, spec, fwd, inv, chunk, devices, whole_in, whole_out, parts):
    length, width = pieces[0].shape[-2:]
    rows = devices * length
    near = pl.BlockSpec(memory_space=pltpu.VMEM)
    far = pl.BlockSpec(memory_space=pl.ANY)
    single = lambda *shape: pltpu.VMEM(shape, jnp.float32)
    half = lambda *shape: pltpu.VMEM(shape, jnp.bfloat16)
    return pl.pallas_call(
        functools.partial(section_kernel, devices, chunk, whole_in, whole_out, parts),
        in_specs=[near] * len(pieces) + [far] + [near] * 3,
        out_specs=[near] * (parts + 1),
        out_shape=[jax.ShapeDtypeStruct((devices // parts, length, width), jnp.bfloat16)] * parts
        + [
            jax.ShapeDtypeStruct((4, rows // 2, width), jnp.bfloat16),
        ],
        scratch_shapes=[
            single(rows + PAD, width),
            single(rows, width),
            single(rows, width),
            single(rows, width),
            half(4, rows // 2, 2 * width),
            half(4, rows // 2, 2 * width),
            single(4, rows // 2, 2 * width),
            single(3, rows + PAD, width),
            half(rows, width),
            single(*taps.shape[1:3], width),
            pltpu.SemaphoreType.DMA,
        ],
        compiler_params=pltpu.CompilerParams(vmem_limit_bytes=SECTION_VMEM),
        cost_estimate=pl.CostEstimate(
            flops=10 * rows * rows * width, bytes_accessed=20 * rows * width, transcendentals=0
        ),
        name="section",
    )(*pieces, taps, spec, fwd, inv)


def filter_kernel(inv_ref, *refs):
    crosses, (filt_ref, back, filt_rows, sem) = refs[:-4], refs[-4:]
    rows, width = filt_rows.shape[1:]
    quarter = rows // 4
    for chunk, cross_ref in enumerate(crosses):
        columns = slice(chunk * width, (chunk + 1) * width)
        for j in range(4):
            back[chunk, j] = jnp.dot(inv_ref[j], cross_ref[j], preferred_element_type=jnp.float32)

        @pl.loop(0, quarter // TILE)
        def _(step):
            begin = pl.multiple_of(step * TILE, TILE)
            real, imag = pl.ds(begin, TILE), pl.ds(begin + quarter, TILE)
            parts = joined(*((back[chunk, j, real, :], back[chunk, j, imag, :]) for j in range(4)))
            for j, part in enumerate(parts):
                filt_rows[chunk, pl.ds(begin + j * quarter, TILE), :] = part * (1.0 / math.sqrt(rows))

        pltpu.make_async_copy(filt_rows.at[chunk], filt_ref.at[:, columns], sem.at[chunk]).start()
    for chunk in range(len(crosses)):
        columns = slice(chunk * width, (chunk + 1) * width)
        pltpu.make_async_copy(filt_rows.at[chunk], filt_ref.at[:, columns], sem.at[chunk]).wait()


def filter_gradient(inv, crosses):
    rows, width = 2 * crosses[0].shape[1], crosses[0].shape[2]
    count = len(crosses)
    return pl.pallas_call(
        filter_kernel,
        in_specs=[pl.BlockSpec(memory_space=pltpu.VMEM)] * (1 + count),
        out_specs=pl.BlockSpec(memory_space=pl.ANY),
        out_shape=jax.ShapeDtypeStruct((rows, width * count), jnp.float32),
        scratch_shapes=[
            pltpu.VMEM((count, 4, rows // 2, width), jnp.float32),
            pltpu.VMEM((count, rows, width), jnp.float32),
            pltpu.SemaphoreType.DMA((count,)),
        ],
        compiler_params=pltpu.CompilerParams(vmem_limit_bytes=FILTER_VMEM),
        cost_estimate=pl.CostEstimate(
            flops=2 * rows * rows * width * count,
            bytes_accessed=6 * rows * width * count,
            transcendentals=0,
        ),
        name="filter",
    )(inv, *crosses)


def phase_table(row_count, col_count, modulus, direction):
    row_ids = lax.broadcasted_iota(jnp.int32, (row_count, col_count), 0)
    col_ids = lax.broadcasted_iota(jnp.int32, (row_count, col_count), 1)
    residue = row_ids * col_ids % modulus
    angles = direction * 2.0 * math.pi / modulus * residue.astype(jnp.float32)
    return (jnp.cos(angles), jnp.sin(angles))


def highest(pattern, first_op, second_op):
    return jnp.einsum(pattern, first_op, second_op, precision=lax.Precision.HIGHEST)


def forward_spectrum(signal, half_q, width_p):
    full_q = 2 * half_q
    blocks = signal.reshape(half_q, width_p, signal.shape[1])
    fq_re, fq_im = phase_table(full_q, half_q, full_q, -1.0)
    section_re = highest("kq,qpc->kpc", fq_re, blocks)
    section_im = highest("kq,qpc->kpc", fq_im, blocks)
    tw_re, tw_im = phase_table(full_q, width_p, full_q * width_p, -1.0)
    turned_re = section_re * tw_re[:, :, None] - section_im * tw_im[:, :, None]
    turned_im = section_re * tw_im[:, :, None] + section_im * tw_re[:, :, None]
    fp_re, fp_im = phase_table(width_p, width_p, width_p, -1.0)
    out_re = highest("jp,kpc->jkc", fp_re, turned_re) - highest("jp,kpc->jkc", fp_im, turned_im)
    out_im = highest("jp,kpc->jkc", fp_re, turned_im) + highest("jp,kpc->jkc", fp_im, turned_re)
    return (out_re, out_im)


def inverse_field(spec_re, spec_im, half_q, width_p):
    full_q = 2 * half_q
    gp_re, gp_im = phase_table(width_p, width_p, width_p, 1.0)
    section_re = highest("mn,nqc->mqc", gp_re, spec_re) - highest("mn,nqc->mqc", gp_im, spec_im)
    section_im = highest("mn,nqc->mqc", gp_re, spec_im) + highest("mn,nqc->mqc", gp_im, spec_re)
    tw_re, tw_im = phase_table(width_p, full_q, full_q * width_p, 1.0)
    turned_re = section_re * tw_re[:, :, None] - section_im * tw_im[:, :, None]
    turned_im = section_re * tw_im[:, :, None] + section_im * tw_re[:, :, None]
    gq_re, gq_im = phase_table(half_q, full_q, full_q, 1.0)
    result = highest("aq,mqc->amc", gq_re, turned_re) - highest("aq,mqc->amc", gq_im, turned_im)
    return result.reshape(half_q * width_p, spec_re.shape[2]) / (full_q * width_p)


def large_section(x, g, taps, kernel, half_q):
    rows = x.shape[0]
    width_p = rows // half_q
    signal, upstream = x.astype(jnp.float32), g.astype(jnp.float32)
    moved = [jnp.pad(signal, ((i, 0), (0, 0)))[:rows] for i in range(3)]
    query, key, value = (
        sum(taps[3 * s + i] * moved[i] for i in range(3)).astype(jnp.bfloat16).astype(jnp.float32)
        for s in range(3)
    )
    p_re, p_im = forward_spectrum(key * value, half_q, width_p)
    a_re, a_im = forward_spectrum(upstream * query, half_q, width_p)
    h_re, h_im = forward_spectrum(kernel, half_q, width_p)
    combined = inverse_field(
        p_re * h_re - p_im * h_im, p_re * h_im + p_im * h_re, half_q, width_p
    )
    backward = inverse_field(
        h_re * a_re + h_im * a_im, h_re * a_im - h_im * a_re, half_q, width_p
    )
    filter_grad = inverse_field(
        p_re * a_re + p_im * a_im, p_re * a_im - p_im * a_re, half_q, width_p
    )
    grads = (upstream * combined, backward * value, backward * key)
    total = jnp.zeros_like(signal)
    for s in range(3):
        grad = grads[s].astype(jnp.bfloat16).astype(jnp.float32)
        for i in range(3):
            total = total + taps[3 * s + i] * jnp.pad(grad, ((0, i), (0, 0)))[i:]
    return total.astype(jnp.bfloat16), filter_grad * (1.0 / math.sqrt(rows))


def exchanged(chunk, devices, whole):
    if whole:
        return [lax.all_to_all(chunk[0], "seq", split_axis=0, concat_axis=0, tiled=True)]
    pairs = lambda k: [(i, i ^ k) for i in range(devices)]
    return [chunk[0]] + [lax.ppermute(chunk[k], "seq", pairs(k)) for k in range(1, devices)]


def fast(inputs, upstream, kernel, taps):
    devices, count = lax.axis_size("seq"), lax.axis_size("pipe")
    before = [(p, (p - 1) % count) for p in range(count)]
    pieces = pack(inputs, upstream, devices, WHOLE_IN)
    fwd, inv = quarter_tables(kernel.shape[0])
    spec = spectrum(kernel, fwd)
    grads, crosses = [], []
    for chunk in range(CHUNKS):
        arrived = exchanged(pieces[chunk], devices, WHOLE_IN[chunk])
        *parts, cross = section(
            arrived, taps, spec, fwd, inv, chunk, devices, WHOLE_IN[chunk], WHOLE_OUT[chunk],
            PARTS[chunk],
        )
        moved = [lax.ppermute(part, "pipe", before) for part in parts[::-1]]
        grads.append(moved[::-1])
        crosses.append(cross)
    filter_grad = filter_gradient(inv, crosses)
    home = []
    for parts, whole in zip(grads, WHOLE_OUT):
        ready = []
        for part in parts:
            part, filter_grad = lax.optimization_barrier((part, filter_grad))
            ready.append(part)
        each = devices // len(ready)
        home.append(
            exchanged(
                ready if whole else [ready[k // each][k % each] for k in range(devices)],
                devices,
                whole,
            )
        )
    return unpack(home, devices, WHOLE_OUT), filter_grad[None]


def general(inputs, upstream, kernel, taps):
    devices, count = lax.axis_size("seq"), lax.axis_size("pipe")
    length_dev, model = inputs.shape
    rows, width = kernel.shape
    to_columns = lambda block: block.reshape(length_dev, devices, width).transpose(1, 0, 2)
    sent = jnp.stack([to_columns(inputs), to_columns(upstream)], axis=1)
    got = lax.all_to_all(sent, "seq", split_axis=0, concat_axis=0, tiled=True)
    x_cols, g_cols = got[:, 0].reshape(rows, width), got[:, 1].reshape(rows, width)
    grad_cols, filter_grad = large_section(x_cols, g_cols, taps, kernel, devices)
    back = lax.all_to_all(
        grad_cols.reshape(devices, length_dev, width), "seq", split_axis=0, concat_axis=0, tiled=True
    )
    grad_input = back.transpose(1, 0, 2).reshape(length_dev, model)
    received = lax.ppermute(
        grad_input[None], "pipe", [((i + 1) % count, i) for i in range(count)]
    )
    return received, filter_grad[None]


def shards(section_input, out_grad, conv_filter, short_taps):
    inputs, upstream, kernel = section_input[0], out_grad[0], conv_filter[0]
    devices = lax.axis_size("seq")
    model = inputs.shape[1]
    rows, width = kernel.shape
    dense = (
        rows <= DENSE_ROWS
        and rows % 256 == 0
        and width % (CHUNKS * 128) == 0
        and devices & (devices - 1) == 0
    )
    if dense:
        return fast(inputs, upstream, kernel, short_taps)
    taps = lax.dynamic_slice_in_dim(
        short_taps[0].reshape(-1, model), lax.axis_index("seq") * width, width, axis=1
    )
    return general(inputs, upstream, kernel, taps)


def solution(mesh):
    return jax.shard_map(
        shards,
        mesh=mesh,
        in_specs=(
            P("pipe", "seq", None),
            P("pipe", "seq", None),
            P("pipe", None, "seq"),
            P("pipe", None, None, None),
        ),
        out_specs=(P("pipe", "seq", None), P("pipe", None, "seq")),
        check_vma=False,
    )
```

```python
import functools
import math

import jax
import jax.numpy as jnp
import numpy as np
from jax import lax
from jax.experimental import pallas as pl
from jax.experimental.pallas import tpu as pltpu
from jax.sharding import PartitionSpec as P

WHOLE_IN = (False, False)
WHOLE_OUT = (True, False)
PARTS = (1, 2)
CHUNKS = len(WHOLE_IN)
PAD = 8
TILE = 16
LAST_TILE = 64
DENSE_ROWS = 1024
SPECTRUM_VMEM = 12 * 1024 * 1024
FILTER_VMEM = 10 * 1024 * 1024
SECTION_VMEM = 21 * 1024 * 1024
COS = [math.cos(math.pi / 8 * j) for j in range(4)]
SIN = [math.sin(math.pi / 8 * j) for j in range(4)]


def quarter_tables(rows):
    quarter = rows // 4
    freqs = 16 * np.arange(quarter)[None, :, None] + 4 * np.arange(4)[:, None, None] + 1
    angles = 2.0 * np.pi / (4 * rows) * (freqs * np.arange(quarter) % (4 * rows))
    real, imag = np.cos(angles), -np.sin(angles)
    fwd = np.concatenate(
        [np.concatenate([real, -imag], axis=2), np.concatenate([imag, real], axis=2)], axis=1
    )
    inv = np.swapaxes(fwd, 1, 2) / rows
    return jnp.asarray(fwd.astype(jnp.bfloat16)), jnp.asarray(inv.astype(jnp.bfloat16))


def split(x0, x1, x2, x3):
    even, turn = x0 + COS[2] * x2, SIN[2] * x2
    odd = x0 - COS[2] * x2
    sum_re, sum_im = COS[1] * x1 + COS[3] * x3, SIN[1] * x1 + SIN[3] * x3
    dif_re, dif_im = COS[1] * x1 - COS[3] * x3, SIN[1] * x1 - SIN[3] * x3
    return (
        (even + sum_re, -turn - sum_im),
        (odd - dif_im, turn - dif_re),
        (even - sum_re, sum_im - turn),
        (odd + dif_im, turn + dif_re),
    )


def joined(v0, v1, v2, v3):
    a_re, a_im, b_re, b_im = v0[0] + v2[0], v0[1] + v2[1], v1[0] + v3[0], v1[1] + v3[1]
    c_re, c_im, d_re, d_im = v0[0] - v2[0], v0[1] - v2[1], v1[0] - v3[0], v1[1] - v3[1]
    return (
        a_re + b_re,
        COS[1] * (c_re - d_im) - SIN[1] * (c_im + d_re),
        COS[2] * (a_re - b_re) - SIN[2] * (a_im - b_im),
        COS[3] * (c_re + d_im) - SIN[3] * (c_im - d_re),
    )


def by_target(refs, devices, whole):
    me, refs = lax.axis_index("seq"), list(refs)
    pairs = []
    for together in whole:
        if together:
            ref = refs.pop(0)
            pairs.append([(d, ref.at[d]) for d in range(devices)])
        else:
            pairs.append([(me ^ k, refs.pop(0)) for k in range(devices)])
    return pairs


def pack_kernel(whole, x_ref, g_ref, *refs):
    pieces, sem = refs[:-1], refs[-1]
    devices = lax.axis_size("seq")
    width = pieces[0].shape[-1]
    copies = []
    for chunk, pairs in enumerate(by_target(pieces, devices, whole)):
        for number, (device, piece) in enumerate(pairs):
            start = pl.multiple_of((device * len(whole) + chunk) * width, width)
            for half, ref in enumerate((x_ref, g_ref)):
                copies.append(
                    pltpu.make_async_copy(
                        ref.at[:, pl.ds(start, width)],
                        piece.at[half],
                        sem.at[chunk * devices + number, half],
                    )
                )
    for copy in copies:
        copy.start()
    for copy in copies:
        copy.wait()


def pack(x, g, devices, whole):
    length, model = x.shape
    width = model // devices // len(whole)
    shapes = []
    for together in whole:
        shapes += [(devices, 2, length, width)] if together else [(2, length, width)] * devices
    pieces = pl.pallas_call(
        functools.partial(pack_kernel, whole),
        in_specs=[pl.BlockSpec(memory_space=pl.ANY)] * 2,
        out_specs=[pl.BlockSpec(memory_space=pltpu.VMEM)] * len(shapes),
        out_shape=[jax.ShapeDtypeStruct(shape, x.dtype) for shape in shapes],
        scratch_shapes=[pltpu.SemaphoreType.DMA((devices * len(whole), 2))],
        compiler_params=pltpu.CompilerParams(vmem_limit_bytes=8 * 1024 * 1024),
        name="pack",
    )(x, g)
    chunks, pieces = [], list(pieces)
    for together in whole:
        taken = 1 if together else devices
        chunks.append(pieces[:taken])
        pieces = pieces[taken:]
    return chunks


def unpack_kernel(whole, *refs):
    pieces, out_ref, sem = refs[:-2], refs[-2], refs[-1]
    devices = lax.axis_size("seq")
    width = pieces[0].shape[-1]
    copies = []
    for chunk, pairs in enumerate(by_target(pieces, devices, whole)):
        for number, (device, piece) in enumerate(pairs):
            start = pl.multiple_of((device * len(whole) + chunk) * width, width)
            copies.append(
                pltpu.make_async_copy(
                    piece,
                    out_ref.at[0, :, pl.ds(start, width)],
                    sem.at[chunk * devices + number],
                )
            )
    for copy in copies:
        copy.start()
    for copy in copies:
        copy.wait()


def unpack(chunks, devices, whole):
    flat = [piece for chunk in chunks for piece in chunk]
    length, width = flat[0].shape[-2:]
    count = devices * len(whole)
    return pl.pallas_call(
        functools.partial(unpack_kernel, whole),
        in_specs=[pl.BlockSpec(memory_space=pltpu.VMEM)] * len(flat),
        out_specs=pl.BlockSpec(memory_space=pl.ANY),
        out_shape=jax.ShapeDtypeStruct((1, length, width * count), flat[0].dtype),
        scratch_shapes=[pltpu.SemaphoreType.DMA((count,))],
        compiler_params=pltpu.CompilerParams(vmem_limit_bytes=8 * 1024 * 1024),
        name="unpack",
    )(*flat)


def spectrum_kernel(kernel_ref, fwd_ref, spec_ref, turned):
    rows = kernel_ref.shape[0]
    quarter = rows // 4

    @pl.loop(0, quarter // TILE, unroll=2)
    def _(step):
        start = pl.multiple_of(step * TILE, TILE)
        parts = split(*(kernel_ref[pl.ds(start + j * quarter, TILE), :] for j in range(4)))
        for j, (real, imag) in enumerate(parts):
            turned[j, pl.ds(start, TILE), :] = real.astype(jnp.bfloat16)
            turned[j, pl.ds(start + quarter, TILE), :] = imag.astype(jnp.bfloat16)

    for j in range(4):
        spec_ref[j] = jnp.dot(fwd_ref[j], turned[j], preferred_element_type=jnp.float32)


def spectrum(kernel, fwd):
    rows, width = kernel.shape
    near = pl.BlockSpec(memory_space=pltpu.VMEM)
    return pl.pallas_call(
        spectrum_kernel,
        in_specs=[near] * 2,
        out_specs=near,
        out_shape=jax.ShapeDtypeStruct((4, rows // 2, width), jnp.float32),
        scratch_shapes=[pltpu.VMEM((4, rows // 2, width), jnp.bfloat16)],
        compiler_params=pltpu.CompilerParams(vmem_limit_bytes=SPECTRUM_VMEM),
        cost_estimate=pl.CostEstimate(
            flops=2 * rows * rows * width, bytes_accessed=14 * rows * width, transcendentals=0
        ),
        name="spectrum",
    )(kernel, fwd)


def section_kernel(devices, chunk, whole_in, whole_out, parts, *refs):
    taken = 1 if whole_in else devices
    (pieces,) = by_target(refs[:taken], devices, [whole_in])
    tap_ref, spec_ref, fwd_ref, inv_ref = refs[taken : taken + 4]
    refs = refs[taken + 4 :]
    out_refs, refs = refs[:parts], refs[parts:]
    cross_ref, refs = refs[0], refs[1:]
    padded, upstream, key_rows, value_rows, turned, mixed, back = refs[:7]
    shifted_rows, grad_rows, tap_rows, tap_sem = refs[7:]
    me = lax.axis_index("seq")
    length, width = pieces[0][1].shape[1:]
    rows = length * devices
    quarter = rows // 4
    columns = slice(chunk * width, (chunk + 1) * width)
    place = lambda device, offset: pl.ds(pl.multiple_of(device * length + offset, 8), length)
    low = lambda v: v

    start = pl.multiple_of((me * (spec_ref.shape[2] // width) + chunk) * width, width)
    fetch = pltpu.make_async_copy(tap_ref.at[0, :, :, pl.ds(start, width)], tap_rows, tap_sem)
    fetch.start()
    padded[0:PAD, :] = jnp.zeros((PAD, width), jnp.float32)
    for device, piece in pieces:
        padded[place(device, PAD), :] = piece[0].astype(jnp.float32)
        upstream[place(device, 0), :] = piece[1].astype(jnp.float32)
    fetch.wait()
    taps = [tap_rows[s, i : i + 1, :] for s in range(3) for i in range(3)]

    @pl.loop(0, quarter // TILE, unroll=2)
    def _(step):
        begin = pl.multiple_of(step * TILE, TILE)
        products, adjoints = [], []
        for j in range(4):
            here = pl.ds(begin + j * quarter, TILE)
            window = padded[pl.ds(begin + j * quarter, TILE + PAD), :]
            moved = [window[PAD - i : PAD - i + TILE, :] for i in range(3)]
            query, key, value = (
                low(sum(taps[3 * s + i] * moved[i] for i in range(3))) for s in range(3)
            )
            key_rows[here, :] = key
            value_rows[here, :] = value
            products.append(key * value)
            adjoints.append(upstream[here, :] * query)
        for number, signals in enumerate((products, adjoints)):
            into = slice(number * width, (number + 1) * width)
            for j, (real, imag) in enumerate(split(*signals)):
                turned[j, pl.ds(begin, TILE), into] = real.astype(jnp.bfloat16)
                turned[j, pl.ds(begin + quarter, TILE), into] = imag.astype(jnp.bfloat16)

    for j in range(4):
        both = jnp.dot(fwd_ref[j], turned[j], preferred_element_type=jnp.float32)
        p_re, p_im = both[:quarter, :width], both[quarter:, :width]
        a_re, a_im = both[:quarter, width:], both[quarter:, width:]
        h_re, h_im = spec_ref[j, :quarter, columns], spec_ref[j, quarter:, columns]
        mixed[j, :quarter, :width] = (p_re * h_re - p_im * h_im).astype(jnp.bfloat16)
        mixed[j, quarter:, :width] = (p_re * h_im + p_im * h_re).astype(jnp.bfloat16)
        mixed[j, :quarter, width:] = (h_re * a_re + h_im * a_im).astype(jnp.bfloat16)
        mixed[j, quarter:, width:] = (h_re * a_im - h_im * a_re).astype(jnp.bfloat16)
        cross_ref[j, :quarter, :] = (p_re * a_re + p_im * a_im).astype(jnp.bfloat16)
        cross_ref[j, quarter:, :] = (p_re * a_im - p_im * a_re).astype(jnp.bfloat16)
        back[j] = jnp.dot(inv_ref[j], mixed[j], preferred_element_type=jnp.float32)

    @pl.loop(0, quarter // TILE, unroll=2)
    def _(step):
        begin = pl.multiple_of(step * TILE, TILE)
        real, imag = pl.ds(begin, TILE), pl.ds(begin + quarter, TILE)
        results = []
        for part in (slice(0, width), slice(width, 2 * width)):
            results.append(joined(*((back[j, real, part], back[j, imag, part]) for j in range(4))))
        for j, (combined, backward) in enumerate(zip(*results)):
            here = pl.ds(begin + j * quarter, TILE)
            grads = (
                low(upstream[here, :] * combined),
                low(backward * value_rows[here, :]),
                low(backward * key_rows[here, :]),
            )
            for i in range(3):
                shifted_rows[i, here, :] = sum(taps[3 * s + i] * grads[s] for s in range(3))

    shifted_rows[:, rows:, :] = jnp.zeros((3, PAD, width), jnp.float32)

    for k in range(devices):
        number, within = divmod(k, devices // parts)
        for offset in range(0, length, LAST_TILE):
            begin = pl.multiple_of((k if whole_out else me ^ k) * length + offset, LAST_TILE)
            windows = [shifted_rows[i, pl.ds(begin, LAST_TILE + PAD), :] for i in range(3)]
            total = sum(windows[i][i : i + LAST_TILE, :] for i in range(3))
            out_refs[number][within, offset : offset + LAST_TILE, :] = total.astype(jnp.bfloat16)


def section(pieces, taps, spec, fwd, inv, chunk, devices, whole_in, whole_out, parts):
    length, width = pieces[0].shape[-2:]
    rows = devices * length
    near = pl.BlockSpec(memory_space=pltpu.VMEM)
    far = pl.BlockSpec(memory_space=pl.ANY)
    single = lambda *shape: pltpu.VMEM(shape, jnp.float32)
    half = lambda *shape: pltpu.VMEM(shape, jnp.bfloat16)
    return pl.pallas_call(
        functools.partial(section_kernel, devices, chunk, whole_in, whole_out, parts),
        in_specs=[near] * len(pieces) + [far] + [near] * 3,
        out_specs=[near] * (parts + 1),
        out_shape=[jax.ShapeDtypeStruct((devices // parts, length, width), jnp.bfloat16)] * parts
        + [
            jax.ShapeDtypeStruct((4, rows // 2, width), jnp.bfloat16),
        ],
        scratch_shapes=[
            single(rows + PAD, width),
            single(rows, width),
            single(rows, width),
            single(rows, width),
            half(4, rows // 2, 2 * width),
            half(4, rows // 2, 2 * width),
            single(4, rows // 2, 2 * width),
            single(3, rows + PAD, width),
            half(rows, width),
            single(*taps.shape[1:3], width),
            pltpu.SemaphoreType.DMA,
        ],
        compiler_params=pltpu.CompilerParams(vmem_limit_bytes=SECTION_VMEM),
        cost_estimate=pl.CostEstimate(
            flops=10 * rows * rows * width, bytes_accessed=20 * rows * width, transcendentals=0
        ),
        name="section",
    )(*pieces, taps, spec, fwd, inv)


def filter_kernel(inv_ref, *refs):
    crosses, (filt_ref, back, filt_rows, sem) = refs[:-4], refs[-4:]
    rows, width = filt_rows.shape[1:]
    quarter = rows // 4
    for chunk, cross_ref in enumerate(crosses):
        columns = slice(chunk * width, (chunk + 1) * width)
        for j in range(4):
            back[chunk, j] = jnp.dot(inv_ref[j], cross_ref[j], preferred_element_type=jnp.float32)

        @pl.loop(0, quarter // TILE, unroll=2)
        def _(step):
            begin = pl.multiple_of(step * TILE, TILE)
            real, imag = pl.ds(begin, TILE), pl.ds(begin + quarter, TILE)
            parts = joined(*((back[chunk, j, real, :], back[chunk, j, imag, :]) for j in range(4)))
            for j, part in enumerate(parts):
                filt_rows[chunk, pl.ds(begin + j * quarter, TILE), :] = part * (1.0 / math.sqrt(rows))

        pltpu.make_async_copy(filt_rows.at[chunk], filt_ref.at[:, columns], sem.at[chunk]).start()
    for chunk in range(len(crosses)):
        columns = slice(chunk * width, (chunk + 1) * width)
        pltpu.make_async_copy(filt_rows.at[chunk], filt_ref.at[:, columns], sem.at[chunk]).wait()


def filter_gradient(inv, crosses):
    rows, width = 2 * crosses[0].shape[1], crosses[0].shape[2]
    count = len(crosses)
    return pl.pallas_call(
        filter_kernel,
        in_specs=[pl.BlockSpec(memory_space=pltpu.VMEM)] * (1 + count),
        out_specs=pl.BlockSpec(memory_space=pl.ANY),
        out_shape=jax.ShapeDtypeStruct((rows, width * count), jnp.float32),
        scratch_shapes=[
            pltpu.VMEM((count, 4, rows // 2, width), jnp.float32),
            pltpu.VMEM((count, rows, width), jnp.float32),
            pltpu.SemaphoreType.DMA((count,)),
        ],
        compiler_params=pltpu.CompilerParams(vmem_limit_bytes=FILTER_VMEM),
        cost_estimate=pl.CostEstimate(
            flops=2 * rows * rows * width * count,
            bytes_accessed=6 * rows * width * count,
            transcendentals=0,
        ),
        name="filter",
    )(inv, *crosses)


def phase_table(row_count, col_count, modulus, direction):
    row_ids = lax.broadcasted_iota(jnp.int32, (row_count, col_count), 0)
    col_ids = lax.broadcasted_iota(jnp.int32, (row_count, col_count), 1)
    residue = row_ids * col_ids % modulus
    angles = direction * 2.0 * math.pi / modulus * residue.astype(jnp.float32)
    return (jnp.cos(angles), jnp.sin(angles))


def highest(pattern, first_op, second_op):
    return jnp.einsum(pattern, first_op, second_op, precision=lax.Precision.HIGHEST)


def forward_spectrum(signal, half_q, width_p):
    full_q = 2 * half_q
    blocks = signal.reshape(half_q, width_p, signal.shape[1])
    fq_re, fq_im = phase_table(full_q, half_q, full_q, -1.0)
    section_re = highest("kq,qpc->kpc", fq_re, blocks)
    section_im = highest("kq,qpc->kpc", fq_im, blocks)
    tw_re, tw_im = phase_table(full_q, width_p, full_q * width_p, -1.0)
    turned_re = section_re * tw_re[:, :, None] - section_im * tw_im[:, :, None]
    turned_im = section_re * tw_im[:, :, None] + section_im * tw_re[:, :, None]
    fp_re, fp_im = phase_table(width_p, width_p, width_p, -1.0)
    out_re = highest("jp,kpc->jkc", fp_re, turned_re) - highest("jp,kpc->jkc", fp_im, turned_im)
    out_im = highest("jp,kpc->jkc", fp_re, turned_im) + highest("jp,kpc->jkc", fp_im, turned_re)
    return (out_re, out_im)


def inverse_field(spec_re, spec_im, half_q, width_p):
    full_q = 2 * half_q
    gp_re, gp_im = phase_table(width_p, width_p, width_p, 1.0)
    section_re = highest("mn,nqc->mqc", gp_re, spec_re) - highest("mn,nqc->mqc", gp_im, spec_im)
    section_im = highest("mn,nqc->mqc", gp_re, spec_im) + highest("mn,nqc->mqc", gp_im, spec_re)
    tw_re, tw_im = phase_table(width_p, full_q, full_q * width_p, 1.0)
    turned_re = section_re * tw_re[:, :, None] - section_im * tw_im[:, :, None]
    turned_im = section_re * tw_im[:, :, None] + section_im * tw_re[:, :, None]
    gq_re, gq_im = phase_table(half_q, full_q, full_q, 1.0)
    result = highest("aq,mqc->amc", gq_re, turned_re) - highest("aq,mqc->amc", gq_im, turned_im)
    return result.reshape(half_q * width_p, spec_re.shape[2]) / (full_q * width_p)


def large_section(x, g, taps, kernel, half_q):
    rows = x.shape[0]
    width_p = rows // half_q
    signal, upstream = x.astype(jnp.float32), g.astype(jnp.float32)
    moved = [jnp.pad(signal, ((i, 0), (0, 0)))[:rows] for i in range(3)]
    query, key, value = (
        sum(taps[3 * s + i] * moved[i] for i in range(3)).astype(jnp.bfloat16).astype(jnp.float32)
        for s in range(3)
    )
    p_re, p_im = forward_spectrum(key * value, half_q, width_p)
    a_re, a_im = forward_spectrum(upstream * query, half_q, width_p)
    h_re, h_im = forward_spectrum(kernel, half_q, width_p)
    combined = inverse_field(
        p_re * h_re - p_im * h_im, p_re * h_im + p_im * h_re, half_q, width_p
    )
    backward = inverse_field(
        h_re * a_re + h_im * a_im, h_re * a_im - h_im * a_re, half_q, width_p
    )
    filter_grad = inverse_field(
        p_re * a_re + p_im * a_im, p_re * a_im - p_im * a_re, half_q, width_p
    )
    grads = (upstream * combined, backward * value, backward * key)
    total = jnp.zeros_like(signal)
    for s in range(3):
        grad = grads[s].astype(jnp.bfloat16).astype(jnp.float32)
        for i in range(3):
            total = total + taps[3 * s + i] * jnp.pad(grad, ((0, i), (0, 0)))[i:]
    return total.astype(jnp.bfloat16), filter_grad * (1.0 / math.sqrt(rows))


def exchanged(chunk, devices, whole):
    if whole:
        return [lax.all_to_all(chunk[0], "seq", split_axis=0, concat_axis=0, tiled=True)]
    pairs = lambda k: [(i, i ^ k) for i in range(devices)]
    return [chunk[0]] + [lax.ppermute(chunk[k], "seq", pairs(k)) for k in range(1, devices)]


def fast(inputs, upstream, kernel, taps):
    devices, count = lax.axis_size("seq"), lax.axis_size("pipe")
    before = [(p, (p - 1) % count) for p in range(count)]
    pieces = pack(inputs, upstream, devices, WHOLE_IN)
    fwd, inv = quarter_tables(kernel.shape[0])
    spec = spectrum(kernel, fwd)
    grads, crosses = [], []
    for chunk in range(CHUNKS):
        arrived = exchanged(pieces[chunk], devices, WHOLE_IN[chunk])
        *parts, cross = section(
            arrived, taps, spec, fwd, inv, chunk, devices, WHOLE_IN[chunk], WHOLE_OUT[chunk],
            PARTS[chunk],
        )
        moved = [lax.ppermute(part, "pipe", before) for part in parts[::-1]]
        grads.append(moved[::-1])
        crosses.append(cross)
    filter_grad = filter_gradient(inv, crosses)
    home = []
    for parts, whole in zip(grads, WHOLE_OUT):
        ready = []
        for part in parts:
            part, filter_grad = lax.optimization_barrier((part, filter_grad))
            ready.append(part)
        each = devices // len(ready)
        home.append(
            exchanged(
                ready if whole else [ready[k // each][k % each] for k in range(devices)],
                devices,
                whole,
            )
        )
    return unpack(home, devices, WHOLE_OUT), filter_grad[None]


def general(inputs, upstream, kernel, taps):
    devices, count = lax.axis_size("seq"), lax.axis_size("pipe")
    length_dev, model = inputs.shape
    rows, width = kernel.shape
    to_columns = lambda block: block.reshape(length_dev, devices, width).transpose(1, 0, 2)
    sent = jnp.stack([to_columns(inputs), to_columns(upstream)], axis=1)
    got = lax.all_to_all(sent, "seq", split_axis=0, concat_axis=0, tiled=True)
    x_cols, g_cols = got[:, 0].reshape(rows, width), got[:, 1].reshape(rows, width)
    grad_cols, filter_grad = large_section(x_cols, g_cols, taps, kernel, devices)
    back = lax.all_to_all(
        grad_cols.reshape(devices, length_dev, width), "seq", split_axis=0, concat_axis=0, tiled=True
    )
    grad_input = back.transpose(1, 0, 2).reshape(length_dev, model)
    received = lax.ppermute(
        grad_input[None], "pipe", [((i + 1) % count, i) for i in range(count)]
    )
    return received, filter_grad[None]


def shards(section_input, out_grad, conv_filter, short_taps):
    inputs, upstream, kernel = section_input[0], out_grad[0], conv_filter[0]
    devices = lax.axis_size("seq")
    model = inputs.shape[1]
    rows, width = kernel.shape
    dense = (
        rows <= DENSE_ROWS
        and rows % 256 == 0
        and width % (CHUNKS * 128) == 0
        and devices & (devices - 1) == 0
    )
    if dense:
        return fast(inputs, upstream, kernel, short_taps)
    taps = lax.dynamic_slice_in_dim(
        short_taps[0].reshape(-1, model), lax.axis_index("seq") * width, width, axis=1
    )
    return general(inputs, upstream, kernel, taps)


def solution(mesh):
    return jax.shard_map(
        shards,
        mesh=mesh,
        in_specs=(
            P("pipe", "seq", None),
            P("pipe", "seq", None),
            P("pipe", None, "seq"),
            P("pipe", None, None, None),
        ),
        out_specs=(P("pipe", "seq", None), P("pipe", None, "seq")),
        check_vma=False,
    )
```

```python
import functools
import math

import jax
import jax.numpy as jnp
import numpy as np
from jax import lax
from jax.experimental import pallas as pl
from jax.experimental.pallas import tpu as pltpu
from jax.sharding import PartitionSpec as P

WHOLE_IN = (False, False)
WHOLE_OUT = (True, False)
LAST_SHARE = 4
CHUNKS = len(WHOLE_IN)
PAD = 8
TILE = 16
LAST_TILE = 64
DENSE_ROWS = 1024
SPECTRUM_VMEM = 12 * 1024 * 1024
FILTER_VMEM = 10 * 1024 * 1024
SECTION_VMEM = 21 * 1024 * 1024
COS = [math.cos(math.pi / 8 * j) for j in range(4)]
SIN = [math.sin(math.pi / 8 * j) for j in range(4)]


def quarter_tables(rows):
    quarter = rows // 4
    freqs = 16 * np.arange(quarter)[None, :, None] + 4 * np.arange(4)[:, None, None] + 1
    angles = 2.0 * np.pi / (4 * rows) * (freqs * np.arange(quarter) % (4 * rows))
    real, imag = np.cos(angles), -np.sin(angles)
    fwd = np.concatenate(
        [np.concatenate([real, -imag], axis=2), np.concatenate([imag, real], axis=2)], axis=1
    )
    inv = np.swapaxes(fwd, 1, 2) / rows
    return jnp.asarray(fwd.astype(jnp.bfloat16)), jnp.asarray(inv.astype(jnp.bfloat16))


def split(x0, x1, x2, x3):
    even, turn = x0 + COS[2] * x2, SIN[2] * x2
    odd = x0 - COS[2] * x2
    sum_re, sum_im = COS[1] * x1 + COS[3] * x3, SIN[1] * x1 + SIN[3] * x3
    dif_re, dif_im = COS[1] * x1 - COS[3] * x3, SIN[1] * x1 - SIN[3] * x3
    return (
        (even + sum_re, -turn - sum_im),
        (odd - dif_im, turn - dif_re),
        (even - sum_re, sum_im - turn),
        (odd + dif_im, turn + dif_re),
    )


def joined(v0, v1, v2, v3):
    a_re, a_im, b_re, b_im = v0[0] + v2[0], v0[1] + v2[1], v1[0] + v3[0], v1[1] + v3[1]
    c_re, c_im, d_re, d_im = v0[0] - v2[0], v0[1] - v2[1], v1[0] - v3[0], v1[1] - v3[1]
    return (
        a_re + b_re,
        COS[1] * (c_re - d_im) - SIN[1] * (c_im + d_re),
        COS[2] * (a_re - b_re) - SIN[2] * (a_im - b_im),
        COS[3] * (c_re + d_im) - SIN[3] * (c_im - d_re),
    )


def by_target(refs, devices, whole):
    me, refs = lax.axis_index("seq"), list(refs)
    pairs = []
    for together in whole:
        if together:
            ref = refs.pop(0)
            pairs.append([(d, ref.at[d]) for d in range(devices)])
        else:
            pairs.append([(me ^ k, refs.pop(0)) for k in range(devices)])
    return pairs


def pack_kernel(whole, x_ref, g_ref, *refs):
    pieces, sem = refs[:-1], refs[-1]
    devices = lax.axis_size("seq")
    width = pieces[0].shape[-1]
    copies = []
    for chunk, pairs in enumerate(by_target(pieces, devices, whole)):
        for number, (device, piece) in enumerate(pairs):
            start = pl.multiple_of((device * len(whole) + chunk) * width, width)
            for half, ref in enumerate((x_ref, g_ref)):
                copies.append(
                    pltpu.make_async_copy(
                        ref.at[:, pl.ds(start, width)],
                        piece.at[half],
                        sem.at[chunk * devices + number, half],
                    )
                )
    for copy in copies:
        copy.start()
    for copy in copies:
        copy.wait()


def pack(x, g, devices, whole):
    length, model = x.shape
    width = model // devices // len(whole)
    shapes = []
    for together in whole:
        shapes += [(devices, 2, length, width)] if together else [(2, length, width)] * devices
    pieces = pl.pallas_call(
        functools.partial(pack_kernel, whole),
        in_specs=[pl.BlockSpec(memory_space=pl.ANY)] * 2,
        out_specs=[pl.BlockSpec(memory_space=pltpu.VMEM)] * len(shapes),
        out_shape=[jax.ShapeDtypeStruct(shape, x.dtype) for shape in shapes],
        scratch_shapes=[pltpu.SemaphoreType.DMA((devices * len(whole), 2))],
        compiler_params=pltpu.CompilerParams(vmem_limit_bytes=8 * 1024 * 1024),
        name="pack",
    )(x, g)
    chunks, pieces = [], list(pieces)
    for together in whole:
        taken = 1 if together else devices
        chunks.append(pieces[:taken])
        pieces = pieces[taken:]
    return chunks


def unpack_kernel(whole, *refs):
    pieces, out_ref, sem = refs[:-2], refs[-2], refs[-1]
    devices = lax.axis_size("seq")
    width = pieces[0].shape[-1]
    copies = []
    for chunk, pairs in enumerate(by_target(pieces, devices, whole)):
        for number, (device, piece) in enumerate(pairs):
            start = pl.multiple_of((device * len(whole) + chunk) * width, width)
            copies.append(
                pltpu.make_async_copy(
                    piece,
                    out_ref.at[0, :, pl.ds(start, width)],
                    sem.at[chunk * devices + number],
                )
            )
    for copy in copies:
        copy.start()
    for copy in copies:
        copy.wait()


def unpack(chunks, devices, whole):
    flat = [piece for chunk in chunks for piece in chunk]
    length, width = flat[0].shape[-2:]
    count = devices * len(whole)
    return pl.pallas_call(
        functools.partial(unpack_kernel, whole),
        in_specs=[pl.BlockSpec(memory_space=pltpu.VMEM)] * len(flat),
        out_specs=pl.BlockSpec(memory_space=pl.ANY),
        out_shape=jax.ShapeDtypeStruct((1, length, width * count), flat[0].dtype),
        scratch_shapes=[pltpu.SemaphoreType.DMA((count,))],
        compiler_params=pltpu.CompilerParams(vmem_limit_bytes=8 * 1024 * 1024),
        name="unpack",
    )(*flat)


def spectrum_kernel(kernel_ref, fwd_ref, spec_ref, turned):
    rows = kernel_ref.shape[0]
    quarter = rows // 4

    @pl.loop(0, quarter // TILE, unroll=2)
    def _(step):
        start = pl.multiple_of(step * TILE, TILE)
        parts = split(*(kernel_ref[pl.ds(start + j * quarter, TILE), :] for j in range(4)))
        for j, (real, imag) in enumerate(parts):
            turned[j, pl.ds(start, TILE), :] = real.astype(jnp.bfloat16)
            turned[j, pl.ds(start + quarter, TILE), :] = imag.astype(jnp.bfloat16)

    for j in range(4):
        spec_ref[j] = jnp.dot(fwd_ref[j], turned[j], preferred_element_type=jnp.float32)


def spectrum(kernel, fwd):
    rows, width = kernel.shape
    near = pl.BlockSpec(memory_space=pltpu.VMEM)
    return pl.pallas_call(
        spectrum_kernel,
        in_specs=[near] * 2,
        out_specs=near,
        out_shape=jax.ShapeDtypeStruct((4, rows // 2, width), jnp.float32),
        scratch_shapes=[pltpu.VMEM((4, rows // 2, width), jnp.bfloat16)],
        compiler_params=pltpu.CompilerParams(vmem_limit_bytes=SPECTRUM_VMEM),
        cost_estimate=pl.CostEstimate(
            flops=2 * rows * rows * width, bytes_accessed=14 * rows * width, transcendentals=0
        ),
        name="spectrum",
    )(kernel, fwd)


def section_kernel(devices, chunk, whole_in, whole_out, parts, *refs):
    taken = 1 if whole_in else devices
    (pieces,) = by_target(refs[:taken], devices, [whole_in])
    tap_ref, spec_ref, fwd_ref, inv_ref = refs[taken : taken + 4]
    refs = refs[taken + 4 :]
    out_refs, refs = refs[: len(parts)], refs[len(parts) :]
    cross_ref, refs = refs[0], refs[1:]
    padded, upstream, key_rows, value_rows, turned, mixed, back = refs[:7]
    shifted_rows, grad_rows, tap_rows, tap_sem = refs[7:]
    me = lax.axis_index("seq")
    length, width = pieces[0][1].shape[1:]
    rows = length * devices
    quarter = rows // 4
    columns = slice(chunk * width, (chunk + 1) * width)
    place = lambda device, offset: pl.ds(pl.multiple_of(device * length + offset, 8), length)
    low = lambda v: v

    start = pl.multiple_of((me * (spec_ref.shape[2] // width) + chunk) * width, width)
    fetch = pltpu.make_async_copy(tap_ref.at[0, :, :, pl.ds(start, width)], tap_rows, tap_sem)
    fetch.start()
    padded[0:PAD, :] = jnp.zeros((PAD, width), jnp.float32)
    for device, piece in pieces:
        padded[place(device, PAD), :] = piece[0].astype(jnp.float32)
        upstream[place(device, 0), :] = piece[1].astype(jnp.float32)
    fetch.wait()
    taps = [tap_rows[s, i : i + 1, :] for s in range(3) for i in range(3)]

    @pl.loop(0, quarter // TILE, unroll=2)
    def _(step):
        begin = pl.multiple_of(step * TILE, TILE)
        products, adjoints = [], []
        for j in range(4):
            here = pl.ds(begin + j * quarter, TILE)
            window = padded[pl.ds(begin + j * quarter, TILE + PAD), :]
            moved = [window[PAD - i : PAD - i + TILE, :] for i in range(3)]
            query, key, value = (
                low(sum(taps[3 * s + i] * moved[i] for i in range(3))) for s in range(3)
            )
            key_rows[here, :] = key
            value_rows[here, :] = value
            products.append(key * value)
            adjoints.append(upstream[here, :] * query)
        for number, signals in enumerate((products, adjoints)):
            into = slice(number * width, (number + 1) * width)
            for j, (real, imag) in enumerate(split(*signals)):
                turned[j, pl.ds(begin, TILE), into] = real.astype(jnp.bfloat16)
                turned[j, pl.ds(begin + quarter, TILE), into] = imag.astype(jnp.bfloat16)

    for j in range(4):
        both = jnp.dot(fwd_ref[j], turned[j], preferred_element_type=jnp.float32)
        p_re, p_im = both[:quarter, :width], both[quarter:, :width]
        a_re, a_im = both[:quarter, width:], both[quarter:, width:]
        h_re, h_im = spec_ref[j, :quarter, columns], spec_ref[j, quarter:, columns]
        mixed[j, :quarter, :width] = (p_re * h_re - p_im * h_im).astype(jnp.bfloat16)
        mixed[j, quarter:, :width] = (p_re * h_im + p_im * h_re).astype(jnp.bfloat16)
        mixed[j, :quarter, width:] = (h_re * a_re + h_im * a_im).astype(jnp.bfloat16)
        mixed[j, quarter:, width:] = (h_re * a_im - h_im * a_re).astype(jnp.bfloat16)
        cross_ref[j, :quarter, :] = (p_re * a_re + p_im * a_im).astype(jnp.bfloat16)
        cross_ref[j, quarter:, :] = (p_re * a_im - p_im * a_re).astype(jnp.bfloat16)
        back[j] = jnp.dot(inv_ref[j], mixed[j], preferred_element_type=jnp.float32)

    @pl.loop(0, quarter // TILE, unroll=2)
    def _(step):
        begin = pl.multiple_of(step * TILE, TILE)
        real, imag = pl.ds(begin, TILE), pl.ds(begin + quarter, TILE)
        results = []
        for part in (slice(0, width), slice(width, 2 * width)):
            results.append(joined(*((back[j, real, part], back[j, imag, part]) for j in range(4))))
        for j, (combined, backward) in enumerate(zip(*results)):
            here = pl.ds(begin + j * quarter, TILE)
            grads = (
                low(upstream[here, :] * combined),
                low(backward * value_rows[here, :]),
                low(backward * key_rows[here, :]),
            )
            for i in range(3):
                shifted_rows[i, here, :] = sum(taps[3 * s + i] * grads[s] for s in range(3))

    shifted_rows[:, rows:, :] = jnp.zeros((3, PAD, width), jnp.float32)

    for k in range(devices):
        number, within = [(n, i) for n, size in enumerate(parts) for i in range(size)][k]
        for offset in range(0, length, LAST_TILE):
            begin = pl.multiple_of((k if whole_out else me ^ k) * length + offset, LAST_TILE)
            windows = [shifted_rows[i, pl.ds(begin, LAST_TILE + PAD), :] for i in range(3)]
            total = sum(windows[i][i : i + LAST_TILE, :] for i in range(3))
            out_refs[number][within, offset : offset + LAST_TILE, :] = total.astype(jnp.bfloat16)


def section(pieces, taps, spec, fwd, inv, chunk, devices, whole_in, whole_out, parts):
    length, width = pieces[0].shape[-2:]
    rows = devices * length
    near = pl.BlockSpec(memory_space=pltpu.VMEM)
    far = pl.BlockSpec(memory_space=pl.ANY)
    single = lambda *shape: pltpu.VMEM(shape, jnp.float32)
    half = lambda *shape: pltpu.VMEM(shape, jnp.bfloat16)
    return pl.pallas_call(
        functools.partial(section_kernel, devices, chunk, whole_in, whole_out, parts),
        in_specs=[near] * len(pieces) + [far] + [near] * 3,
        out_specs=[near] * (len(parts) + 1),
        out_shape=[jax.ShapeDtypeStruct((size, length, width), jnp.bfloat16) for size in parts]
        + [
            jax.ShapeDtypeStruct((4, rows // 2, width), jnp.bfloat16),
        ],
        scratch_shapes=[
            single(rows + PAD, width),
            single(rows, width),
            single(rows, width),
            single(rows, width),
            half(4, rows // 2, 2 * width),
            half(4, rows // 2, 2 * width),
            single(4, rows // 2, 2 * width),
            single(3, rows + PAD, width),
            half(rows, width),
            single(*taps.shape[1:3], width),
            pltpu.SemaphoreType.DMA,
        ],
        compiler_params=pltpu.CompilerParams(vmem_limit_bytes=SECTION_VMEM),
        cost_estimate=pl.CostEstimate(
            flops=10 * rows * rows * width, bytes_accessed=20 * rows * width, transcendentals=0
        ),
        name="section",
    )(*pieces, taps, spec, fwd, inv)


def filter_kernel(inv_ref, *refs):
    crosses, (filt_ref, back, filt_rows, sem) = refs[:-4], refs[-4:]
    rows, width = filt_rows.shape[1:]
    quarter = rows // 4
    for chunk, cross_ref in enumerate(crosses):
        columns = slice(chunk * width, (chunk + 1) * width)
        for j in range(4):
            back[chunk, j] = jnp.dot(inv_ref[j], cross_ref[j], preferred_element_type=jnp.float32)

        @pl.loop(0, quarter // TILE, unroll=2)
        def _(step):
            begin = pl.multiple_of(step * TILE, TILE)
            real, imag = pl.ds(begin, TILE), pl.ds(begin + quarter, TILE)
            parts = joined(*((back[chunk, j, real, :], back[chunk, j, imag, :]) for j in range(4)))
            for j, part in enumerate(parts):
                filt_rows[chunk, pl.ds(begin + j * quarter, TILE), :] = part * (1.0 / math.sqrt(rows))

        pltpu.make_async_copy(filt_rows.at[chunk], filt_ref.at[:, columns], sem.at[chunk]).start()
    for chunk in range(len(crosses)):
        columns = slice(chunk * width, (chunk + 1) * width)
        pltpu.make_async_copy(filt_rows.at[chunk], filt_ref.at[:, columns], sem.at[chunk]).wait()


def filter_gradient(inv, crosses):
    rows, width = 2 * crosses[0].shape[1], crosses[0].shape[2]
    count = len(crosses)
    return pl.pallas_call(
        filter_kernel,
        in_specs=[pl.BlockSpec(memory_space=pltpu.VMEM)] * (1 + count),
        out_specs=pl.BlockSpec(memory_space=pl.ANY),
        out_shape=jax.ShapeDtypeStruct((rows, width * count), jnp.float32),
        scratch_shapes=[
            pltpu.VMEM((count, 4, rows // 2, width), jnp.float32),
            pltpu.VMEM((count, rows, width), jnp.float32),
            pltpu.SemaphoreType.DMA((count,)),
        ],
        compiler_params=pltpu.CompilerParams(vmem_limit_bytes=FILTER_VMEM),
        cost_estimate=pl.CostEstimate(
            flops=2 * rows * rows * width * count,
            bytes_accessed=6 * rows * width * count,
            transcendentals=0,
        ),
        name="filter",
    )(inv, *crosses)


def phase_table(row_count, col_count, modulus, direction):
    row_ids = lax.broadcasted_iota(jnp.int32, (row_count, col_count), 0)
    col_ids = lax.broadcasted_iota(jnp.int32, (row_count, col_count), 1)
    residue = row_ids * col_ids % modulus
    angles = direction * 2.0 * math.pi / modulus * residue.astype(jnp.float32)
    return (jnp.cos(angles), jnp.sin(angles))


def highest(pattern, first_op, second_op):
    return jnp.einsum(pattern, first_op, second_op, precision=lax.Precision.HIGHEST)


def forward_spectrum(signal, half_q, width_p):
    full_q = 2 * half_q
    blocks = signal.reshape(half_q, width_p, signal.shape[1])
    fq_re, fq_im = phase_table(full_q, half_q, full_q, -1.0)
    section_re = highest("kq,qpc->kpc", fq_re, blocks)
    section_im = highest("kq,qpc->kpc", fq_im, blocks)
    tw_re, tw_im = phase_table(full_q, width_p, full_q * width_p, -1.0)
    turned_re = section_re * tw_re[:, :, None] - section_im * tw_im[:, :, None]
    turned_im = section_re * tw_im[:, :, None] + section_im * tw_re[:, :, None]
    fp_re, fp_im = phase_table(width_p, width_p, width_p, -1.0)
    out_re = highest("jp,kpc->jkc", fp_re, turned_re) - highest("jp,kpc->jkc", fp_im, turned_im)
    out_im = highest("jp,kpc->jkc", fp_re, turned_im) + highest("jp,kpc->jkc", fp_im, turned_re)
    return (out_re, out_im)


def inverse_field(spec_re, spec_im, half_q, width_p):
    full_q = 2 * half_q
    gp_re, gp_im = phase_table(width_p, width_p, width_p, 1.0)
    section_re = highest("mn,nqc->mqc", gp_re, spec_re) - highest("mn,nqc->mqc", gp_im, spec_im)
    section_im = highest("mn,nqc->mqc", gp_re, spec_im) + highest("mn,nqc->mqc", gp_im, spec_re)
    tw_re, tw_im = phase_table(width_p, full_q, full_q * width_p, 1.0)
    turned_re = section_re * tw_re[:, :, None] - section_im * tw_im[:, :, None]
    turned_im = section_re * tw_im[:, :, None] + section_im * tw_re[:, :, None]
    gq_re, gq_im = phase_table(half_q, full_q, full_q, 1.0)
    result = highest("aq,mqc->amc", gq_re, turned_re) - highest("aq,mqc->amc", gq_im, turned_im)
    return result.reshape(half_q * width_p, spec_re.shape[2]) / (full_q * width_p)


def large_section(x, g, taps, kernel, half_q):
    rows = x.shape[0]
    width_p = rows // half_q
    signal, upstream = x.astype(jnp.float32), g.astype(jnp.float32)
    moved = [jnp.pad(signal, ((i, 0), (0, 0)))[:rows] for i in range(3)]
    query, key, value = (
        sum(taps[3 * s + i] * moved[i] for i in range(3)).astype(jnp.bfloat16).astype(jnp.float32)
        for s in range(3)
    )
    p_re, p_im = forward_spectrum(key * value, half_q, width_p)
    a_re, a_im = forward_spectrum(upstream * query, half_q, width_p)
    h_re, h_im = forward_spectrum(kernel, half_q, width_p)
    combined = inverse_field(
        p_re * h_re - p_im * h_im, p_re * h_im + p_im * h_re, half_q, width_p
    )
    backward = inverse_field(
        h_re * a_re + h_im * a_im, h_re * a_im - h_im * a_re, half_q, width_p
    )
    filter_grad = inverse_field(
        p_re * a_re + p_im * a_im, p_re * a_im - p_im * a_re, half_q, width_p
    )
    grads = (upstream * combined, backward * value, backward * key)
    total = jnp.zeros_like(signal)
    for s in range(3):
        grad = grads[s].astype(jnp.bfloat16).astype(jnp.float32)
        for i in range(3):
            total = total + taps[3 * s + i] * jnp.pad(grad, ((0, i), (0, 0)))[i:]
    return total.astype(jnp.bfloat16), filter_grad * (1.0 / math.sqrt(rows))


def exchanged(chunk, devices, whole):
    if whole:
        return [lax.all_to_all(chunk[0], "seq", split_axis=0, concat_axis=0, tiled=True)]
    pairs = lambda k: [(i, i ^ k) for i in range(devices)]
    return [chunk[0]] + [lax.ppermute(chunk[k], "seq", pairs(k)) for k in range(1, devices)]


def parts_of(devices):
    return (devices,), (devices - devices // LAST_SHARE, devices // LAST_SHARE)


def fast(inputs, upstream, kernel, taps):
    devices, count = lax.axis_size("seq"), lax.axis_size("pipe")
    before = [(p, (p - 1) % count) for p in range(count)]
    pieces = pack(inputs, upstream, devices, WHOLE_IN)
    fwd, inv = quarter_tables(kernel.shape[0])
    spec = spectrum(kernel, fwd)
    grads, crosses = [], []
    for chunk in range(CHUNKS):
        arrived = exchanged(pieces[chunk], devices, WHOLE_IN[chunk])
        *parts, cross = section(
            arrived, taps, spec, fwd, inv, chunk, devices, WHOLE_IN[chunk], WHOLE_OUT[chunk],
            parts_of(devices)[chunk],
        )
        moved = [lax.ppermute(part, "pipe", before) for part in parts[::-1]]
        grads.append(moved[::-1])
        crosses.append(cross)
    filter_grad = filter_gradient(inv, crosses)
    home = []
    for parts, whole in zip(grads, WHOLE_OUT):
        ready = []
        for part in parts:
            part, filter_grad = lax.optimization_barrier((part, filter_grad))
            ready.append(part)
        split_up = [part[i] for part in ready for i in range(part.shape[0])]
        home.append(
            exchanged(
                ready if whole else split_up,
                devices,
                whole,
            )
        )
    return unpack(home, devices, WHOLE_OUT), filter_grad[None]


def general(inputs, upstream, kernel, taps):
    devices, count = lax.axis_size("seq"), lax.axis_size("pipe")
    length_dev, model = inputs.shape
    rows, width = kernel.shape
    to_columns = lambda block: block.reshape(length_dev, devices, width).transpose(1, 0, 2)
    sent = jnp.stack([to_columns(inputs), to_columns(upstream)], axis=1)
    got = lax.all_to_all(sent, "seq", split_axis=0, concat_axis=0, tiled=True)
    x_cols, g_cols = got[:, 0].reshape(rows, width), got[:, 1].reshape(rows, width)
    grad_cols, filter_grad = large_section(x_cols, g_cols, taps, kernel, devices)
    back = lax.all_to_all(
        grad_cols.reshape(devices, length_dev, width), "seq", split_axis=0, concat_axis=0, tiled=True
    )
    grad_input = back.transpose(1, 0, 2).reshape(length_dev, model)
    received = lax.ppermute(
        grad_input[None], "pipe", [((i + 1) % count, i) for i in range(count)]
    )
    return received, filter_grad[None]


def shards(section_input, out_grad, conv_filter, short_taps):
    inputs, upstream, kernel = section_input[0], out_grad[0], conv_filter[0]
    devices = lax.axis_size("seq")
    model = inputs.shape[1]
    rows, width = kernel.shape
    dense = (
        rows <= DENSE_ROWS
        and rows % 256 == 0
        and width % (CHUNKS * 128) == 0
        and devices & (devices - 1) == 0
    )
    if dense:
        return fast(inputs, upstream, kernel, short_taps)
    taps = lax.dynamic_slice_in_dim(
        short_taps[0].reshape(-1, model), lax.axis_index("seq") * width, width, axis=1
    )
    return general(inputs, upstream, kernel, taps)


def solution(mesh):
    return jax.shard_map(
        shards,
        mesh=mesh,
        in_specs=(
            P("pipe", "seq", None),
            P("pipe", "seq", None),
            P("pipe", None, "seq"),
            P("pipe", None, None, None),
        ),
        out_specs=(P("pipe", "seq", None), P("pipe", None, "seq")),
        check_vma=False,
    )
```
